768 devices in a mesh: dom: 96 (over y, z), feat: 8 (over x, core).
Axes of the slice: x: 4, y: 8, z: 12, core: 2. Of those that a mesh axis runs over, the one named last changes fastest.
Arguments:
- features: bfloat16 [98304, 512], P('dom', 'feat'), may hold values from -6 to 6
- w_self: bfloat16 [512, 512], P('feat'), may hold values from -0.25 to 0.25
- w_neigh: bfloat16 [512, 512], P('feat'), may hold values from -0.25 to 0.25
- degree: int32 [98304], P('dom'), may hold values from 1 to 32
- local_vals: bfloat16 [96, 16, 128, 128], P('dom'), may hold values from 0 to 0.19921875
- local_dst: int32 [96, 16], P('dom'), may hold values from 0 to 7
- local_src: int32 [96, 16], P('dom'), may hold values from 0 to 7
- remote_vals: bfloat16 [96, 6, 8, 128, 128], P('dom'), may hold values from 0 to 0.19921875
- remote_dst: int32 [96, 6, 8], P('dom'), may hold values from 0 to 7
- remote_src: int32 [96, 6, 8], P('dom'), may hold values from 0 to 7
- cotangent: bfloat16 [98304, 512], P('dom', 'feat'), may hold values from -6 to 6
Outputs:
- out: bfloat16 [98304, 512], P('dom', 'feat')
- grad_x: float32 [98304, 512], P('dom', 'feat')
- grad_self: float32 [512, 512], P('feat')
- grad_neigh: float32 [512, 512], P('feat')
The draws below stay inside these ranges and needn't reach their ends.
All inputs are finite; a program needn't handle non-finite values.
Results may differ from the reference program's by a relative error of at most 0.0068.
Values may be sent and summed in bfloat16 or wider, within the bound.
A program may use at most 32 MiB of HBM per device.

```python
import jax
import jax.numpy as jnp
from jax import lax

D = 512
BLK = 128
RB = 8
LT = 16
ROUNDS = 6
K = 8
NODES = 98304
N_DOM = 96


def place_ends(drawn, rng, least, high):
    extent = drawn.shape
    index_at = [jax.random.randint(jax.random.fold_in(rng, axis), (), 0, extent[axis]) for axis in range(len(extent))]
    drawn = drawn.at[tuple(index_at)].set(least)
    longest = extent.index(max(extent))
    index_at[longest] = (index_at[longest] + 1) % extent[longest]
    return drawn.at[tuple(index_at)].set(high)


def level_of(own_key, dims, split, least, largest):
    factor_of = 1.0
    for dim, blocks in split:
        heights = jax.random.uniform(jax.random.fold_in(jax.random.fold_in(own_key, 6), dim), (blocks,), jnp.float32, least / len(split), largest / len(split))
        factor_of = factor_of * jnp.repeat(jnp.exp(heights), dims[dim] // blocks).reshape((-1,) + (1,) * (len(dims) - 1 - dim))
    return factor_of


def gaussian(stream_key, extent, deviation, reach, shards=(), held_as=jnp.bfloat16):
    array = deviation * jax.random.normal(stream_key, extent, jnp.float32)
    if shards:
        array = array * level_of(stream_key, extent, shards, -0.22, 0.18)
    return jnp.clip(array, -reach, reach).astype(held_as)


def setup_inputs(seed: int = 0) -> dict:
    arg_keys = jax.random.split(jax.random.key(seed), 12)
    features = gaussian(arg_keys[0], (NODES, D), 1.0, 6.0, ((0, 96), (1, 8)))
    w_self = gaussian(arg_keys[1], (D, D), D ** -0.5, 0.25, ((0, 8),))
    w_neigh = gaussian(arg_keys[2], (D, D), D ** -0.5, 0.25, ((0, 8),))
    degree = place_ends(jax.random.randint(arg_keys[3], (NODES,), 1, 33), jax.random.fold_in(arg_keys[3], 1), 1, 32).astype(jnp.int32)
    local_vals = jnp.clip(0.19921875 * jax.random.uniform(arg_keys[4], (N_DOM, LT, BLK, BLK), jnp.float32) ** level_of(arg_keys[4], (N_DOM, LT, BLK, BLK), ((0, 96),), -0.2, 0.2), 0.0, 0.19921875).astype(jnp.bfloat16)
    local_dst = place_ends(jax.random.randint(arg_keys[5], (N_DOM, LT), 0, RB), jax.random.fold_in(arg_keys[5], 1), 0, RB - 1).astype(jnp.int32)
    local_src = place_ends(jax.random.randint(arg_keys[6], (N_DOM, LT), 0, RB), jax.random.fold_in(arg_keys[6], 1), 0, RB - 1).astype(jnp.int32)
    remote_vals = jnp.clip(0.19921875 * jax.random.uniform(arg_keys[7], (N_DOM, ROUNDS, K, BLK, BLK), jnp.float32) ** level_of(arg_keys[7], (N_DOM, ROUNDS, K, BLK, BLK), ((0, 96),), -0.2, 0.2), 0.0, 0.19921875).astype(jnp.bfloat16)
    remote_dst = place_ends(jax.random.randint(arg_keys[8], (N_DOM, ROUNDS, K), 0, RB), jax.random.fold_in(arg_keys[8], 1), 0, RB - 1).astype(jnp.int32)
    remote_src = place_ends(jax.random.randint(arg_keys[9], (N_DOM, ROUNDS, K), 0, RB), jax.random.fold_in(arg_keys[9], 1), 0, RB - 1).astype(jnp.int32)
    cotangent = gaussian(arg_keys[10], (NODES, D), 1.0, 6.0, ((0, 96), (1, 8)))
    return {"features": features, "w_self": w_self, "w_neigh": w_neigh, "degree": degree, "local_vals": local_vals, "local_dst": local_dst, "local_src": local_src, "remote_vals": remote_vals, "remote_dst": remote_dst, "remote_src": remote_src, "cotangent": cotangent}


def onehot(block_ids):
    return (block_ids[:, None] == jnp.arange(RB, dtype=jnp.int32)[None, :]).astype(jnp.float32)


def tile_apply(tiles, blocks):
    return jnp.einsum("kij,kjf->kif", tiles.astype(jnp.float32), blocks.astype(jnp.float32), precision=lax.Precision.HIGHEST)


def tile_apply_back(tiles, blocks):
    return jnp.einsum("kji,kjf->kif", tiles.astype(jnp.float32), blocks.astype(jnp.float32), precision=lax.Precision.HIGHEST)


def spread(parts, block_ids):
    return jnp.einsum("kc,kif->cif", onehot(block_ids), parts, precision=lax.Precision.HIGHEST)


def reference(features, w_self, w_neigh, degree, local_vals, local_dst, local_src, remote_vals, remote_dst, remote_src, cotangent):
    offsets = [(step + 1) * N_DOM // (ROUNDS + 1) for step in range(ROUNDS)]
    blocks = features.reshape(N_DOM, RB, BLK, D)

    def forward_sum(part):
        totals = spread(tile_apply(local_vals[part], blocks[part][local_src[part]]), local_dst[part])
        for step in range(ROUNDS):
            source = (part - offsets[step]) % N_DOM
            piece = tile_apply(remote_vals[source, step], blocks[source][remote_src[source, step]])
            piece = lax.optimization_barrier(piece.astype(jnp.bfloat16)).astype(jnp.float32)
            totals = totals + spread(piece, remote_dst[source, step])
        return totals

    sums = lax.map(forward_sum, jnp.arange(N_DOM, dtype=jnp.int32))
    inverse = 1.0 / degree.astype(jnp.float32)
    agg = (sums.reshape(NODES, D) * inverse[:, None]).astype(jnp.bfloat16)
    pre = jnp.dot(features, w_self, preferred_element_type=jnp.float32) + jnp.dot(agg, w_neigh, preferred_element_type=jnp.float32)
    sigma = jax.nn.sigmoid(pre)
    out = (pre * sigma).astype(jnp.bfloat16)
    dpre = (cotangent.astype(jnp.float32) * sigma * (1.0 + pre * (1.0 - sigma))).astype(jnp.bfloat16)
    grad_self = jnp.dot(features.T, dpre, preferred_element_type=jnp.float32)
    grad_neigh = jnp.dot(agg.T, dpre, preferred_element_type=jnp.float32)
    dx_self = jnp.dot(dpre, w_self.T, preferred_element_type=jnp.float32)
    dagg = jnp.dot(dpre, w_neigh.T, preferred_element_type=jnp.float32)
    dsum = (dagg * inverse[:, None]).astype(jnp.bfloat16).reshape(N_DOM, RB, BLK, D)

    def backward_sum(part):
        totals = spread(tile_apply_back(local_vals[part], dsum[part][local_dst[part]]), local_src[part])
        for step in range(ROUNDS):
            target = (part + offsets[step]) % N_DOM
            picked = dsum[target][remote_dst[part, step]]
            totals = totals + spread(tile_apply_back(remote_vals[part, step], picked), remote_src[part, step])
        return totals

    back = lax.map(backward_sum, jnp.arange(N_DOM, dtype=jnp.int32))
    grad_x = dx_self + back.reshape(NODES, D)
    return (out, grad_x, grad_self, grad_neigh)
```

```python
import functools

import jax
import jax.numpy as jnp
from jax import lax
from jax.experimental import pallas as pl
from jax.experimental.pallas import tpu as pltpu
from jax.sharding import PartitionSpec as P

Z_CHIPS = 12
CORES = 2
MESH = pl.DeviceIdType.MESH
F32 = jnp.float32
BF16 = jnp.bfloat16


def kernel(
    nd,
    nf,
    offsets,
    ld,
    ls,
    rd,
    rs,
    xt,
    ct,
    ws,
    wn,
    deg,
    lv,
    rv,
    out,
    gx,
    gs,
    gn,
    xb,
    accs,
    loc,
    parts,
    psend,
    precv,
    wt,
    wrecv,
    wsn,
    xfull,
    afull,
    dfull,
    dsb,
    dr0,
    dr1,
    dr2,
    dr3,
    dr4,
    dr5,
    gsend,
    gyrecv,
    gz,
    gfin,
    pre,
    fs,
    fr,
    bs,
    br,
    wss,
    wsr,
    xs,
    xr,
    as_,
    ar,
    ds,
    dr,
    gys,
    gyr,
    gzs,
    gzr,
    gas,
    gar,
):
    width, rows = xt.shape
    nb = xb.shape[0]
    blk = xb.shape[2]
    drecv = [dr0, dr1, dr2, dr3, dr4, dr5]
    per = rv.shape[1]
    nz = Z_CHIPS
    ny = nd // nz
    nx = nf // CORES
    o = offsets
    me = lax.axis_index("dom")
    f = lax.axis_index("feat")
    y, z = me // nz, me % nz
    x, c = f // CORES, f % CORES
    f_sib = x * CORES + (CORES - 1 - c)
    f_left = ((x + nx - 1) % nx) * CORES + c
    f_right = ((x + 1) % nx) * CORES + c
    f_opp = ((x + 2) % nx) * CORES + c

    def dom_at(by):
        return (me + by + nd) % nd

    up = [o[2] - o[1], o[1] - o[0], o[0]]
    down = [o[4] - o[3], o[5] - o[4], nd - o[5]]

    barrier = pltpu.get_barrier_semaphore()
    near = sorted({h % nd for h in up + down} | {(nd - h) % nd for h in up + down})
    partners = [(dom_at(h), f) for h in near]
    partners += [(me, (f + k) % nf) for k in range(1, nf)]
    partners += [(y * nz + (z + k) % nz, f) for k in range(1, nz)]
    partners += [(((y + k) % ny) * nz + z, f) for k in range(1, ny)]
    for partner in partners:
        pl.semaphore_signal(barrier, inc=1, device_id=partner, device_id_type=MESH)

    def push(src, dst, send, recv, dom, feat):
        copy = pltpu.make_async_remote_copy(
            src_ref=src,
            dst_ref=dst,
            send_sem=send,
            recv_sem=recv,
            device_id=(dom, feat),
            device_id_type=MESH,
        )
        copy.start()
        return copy

    def collect(vals, first, pick, put, blocks, dims, acc):
        for t in range(per):
            parts[t] = lax.dot_general(
                blocks[pick[t]], vals[first + t], dims, preferred_element_type=F32
            )
        for b in range(nb):
            total = jnp.zeros((width, blk), F32)
            for t in range(per):
                total = total + jnp.where(put[t] == b, parts[t], 0.0)
            acc(b, total)

    def remote_forward(r, acc):
        collect(
            rv.at[r],
            0,
            [rs[r, t] for t in range(per)],
            [rd[r, t] for t in range(per)],
            xb,
            (((1,), (1,)), ((), ())),
            acc,
        )

    def to_send(k):
        def put(b, total):
            psend[k, b] = total.astype(BF16)

        return put

    def to_acc(k):
        def put(b, total):
            accs[k, b] = total

        return put

    for b in range(nb):
        xb[b] = xt[:, b * blk : (b + 1) * blk]
    remote_forward(2, to_send(0))
    remote_forward(3, to_send(1))
    pl.semaphore_wait(barrier, len(partners))

    fwd = [None] * 6
    fwd[0] = push(psend.at[0], precv.at[0], fs.at[0], fr.at[0], dom_at(up[0]), f)
    fwd[1] = push(psend.at[1], precv.at[1], fs.at[1], fr.at[1], dom_at(-down[0]), f)

    xfull[f] = xt[...]
    early = []
    for k in range(1, nf):
        to = (f + k) % nf
        early.append(push(xt, xfull.at[f], xs.at[k], xr.at[k], me, to))
    for q in range(ws.shape[1] // blk):
        cols = jnp.concatenate(
            [ws[:, q * blk : (q + 1) * blk], wn[:, q * blk : (q + 1) * blk]], axis=0
        )
        turned = cols.T
        for h in range(blk // width):
            wt[q * (blk // width) + h] = turned[h * width : (h + 1) * width]
    wrecv[f] = wt[f]
    for k in range(1, nf):
        to = (f + k) % nf
        early.append(push(wt.at[to], wrecv.at[f], wss.at[k], wsr.at[k], me, to))

    remote_forward(1, to_acc(0))
    remote_forward(4, to_acc(1))
    for side, hop in ((0, up[1]), (1, -down[1])):
        fwd[side].wait_recv()
        psend[2 + side] = (accs[side] + precv[side].astype(F32)).astype(BF16)
        k = 2 + side
        fwd[k] = push(psend.at[k], precv.at[k], fs.at[k], fr.at[k], dom_at(hop), f)
    remote_forward(0, to_acc(0))
    remote_forward(5, to_acc(1))
    for side, hop in ((0, up[2]), (1, -down[2])):
        fwd[2 + side].wait_recv()
        k = 4 + side
        psend[k] = (accs[side] + precv[2 + side].astype(F32)).astype(BF16)
        fwd[k] = push(psend.at[k], precv.at[k], fs.at[k], fr.at[k], dom_at(hop), f)

    def to_loc(b, total):
        loc[b] = total

    def add_loc(b, total):
        loc[b] = loc[b] + total

    for g in range(lv.shape[0] // per):
        collect(
            lv,
            g * per,
            [ls[0, g * per + t] for t in range(per)],
            [ld[0, g * per + t] for t in range(per)],
            xb,
            (((1,), (1,)), ((), ())),
            add_loc if g else to_loc,
        )
    for copy in early:
        copy.wait_recv()
    pair = blk // width
    for half, dst in ((0, 0), (1, 1)):
        for q in range(nf // pair):
            wsn[dst, :, q * blk : (q + 1) * blk] = jnp.concatenate(
                [wrecv[q * pair + h][:, half * width : (half + 1) * width] for h in range(pair)],
                axis=1,
            )
    pre[...] = jnp.dot(
        wsn[0], xfull[...].reshape(nf * width, rows), preferred_element_type=F32
    )
    inverse = 1.0 / deg[...].astype(F32)
    fwd[4].wait_recv()
    fwd[5].wait_recv()
    for b in range(nb):
        sums = loc[b] + precv[4, b].astype(F32) + precv[5, b].astype(F32)
        afull[f, :, b * blk : (b + 1) * blk] = (
            sums * inverse[:, b * blk : (b + 1) * blk]
        ).astype(BF16)

    half = width // 2

    def gather(full, send, recv):
        def go(k, which, feat, low=0, size=width):
            part = full.at[which, pl.ds(low, size)]
            return push(part, part, send.at[k], recv.at[k], me, feat)

        if nx == 1:
            copy = go(0, f, f_sib)
            copy.wait()
            return
        sent = [go(1, f, f_right), go(2, f, f_left), go(0, f, f_sib)]
        sent[0].wait_recv()
        sent.append(go(4, f_left, f_right, 0, half))
        sent.append(go(3, f_left, f_sib))
        sent[1].wait_recv()
        sent.append(go(6, f_right, f_left, half, half))
        sent.append(go(5, f_right, f_sib))
        sent[3].wait_recv()
        sent.append(go(7, f_opp, f_sib, 0, half))
        sent[5].wait_recv()
        sent.append(go(8, f_opp, f_sib, half, half))
        for k in (2, 4, 6, 7, 8):
            sent[k].wait_recv()
        for copy in sent:
            copy.wait_send()

    gather(afull, as_, ar)
    total = pre[...] + jnp.dot(
        wsn[1], afull[...].reshape(nf * width, rows), preferred_element_type=F32
    )
    sigma = 1.0 / (1.0 + jnp.exp(-total))
    out[...] = (total * sigma).astype(BF16)
    dfull[f] = (ct[...].astype(F32) * sigma * (1.0 + total * (1.0 - sigma))).astype(BF16)

    gather(dfull, ds, dr)
    dall = dfull[...].reshape(nf * width, rows)
    dagg = jnp.dot(wn[...], dall, preferred_element_type=F32)
    for b in range(nb):
        dsb[b] = (
            dagg[:, b * blk : (b + 1) * blk] * inverse[:, b * blk : (b + 1) * blk]
        ).astype(BF16)

    back = [None] * 6
    back_down = [o[0], o[1] - o[0], o[2] - o[1]]
    back_up = [nd - o[5], o[5] - o[4], o[4] - o[3]]
    back[0] = push(dsb, drecv[0], bs.at[0], br.at[0], dom_at(-back_down[0]), f)
    back[1] = push(dsb, drecv[1], bs.at[1], br.at[1], dom_at(back_up[0]), f)

    gx[...] = jnp.dot(ws[...], dall, preferred_element_type=F32)
    grad = lax.dot_general(
        jnp.concatenate([xt[...], afull[f]], axis=0),
        dall,
        (((1,), (1,)), ((), ())),
        preferred_element_type=F32,
    )
    slab = gsend.shape[1]
    for k in range(ny):
        gsend[k] = grad[k * slab : (k + 1) * slab].astype(BF16)
    gyrecv[y] = gsend[y]
    gy_copies = []
    for k in range(1, ny):
        to = (y + k) % ny
        gy_copies.append(
            push(gsend.at[to], gyrecv.at[y], gys.at[k], gyr.at[k], to * nz + z, f)
        )

    def add_gx(b, total):
        gx[:, b * blk : (b + 1) * blk] = gx[:, b * blk : (b + 1) * blk] + total

    nn = (((1,), (0,)), ((), ()))
    for g in range(lv.shape[0] // per):
        collect(
            lv,
            g * per,
            [ld[0, g * per + t] for t in range(per)],
            [ls[0, g * per + t] for t in range(per)],
            dsb,
            nn,
            add_gx,
        )

    def remote_back(r, k):
        collect(
            rv.at[r],
            0,
            [rd[r, t] for t in range(per)],
            [rs[r, t] for t in range(per)],
            drecv[k],
            nn,
            add_gx,
        )

    def relay(k, hop):
        back[k].wait_recv()
        if k < 4:
            n = k + 2
            back[n] = push(drecv[k], drecv[n], bs.at[n], br.at[n], dom_at(hop), f)

    relay(0, -back_down[1])
    relay(1, back_up[1])
    for copy in gy_copies:
        copy.wait_recv()
    mine = gyrecv[0].astype(F32)
    for k in range(1, ny):
        mine = mine + gyrecv[k].astype(F32)
    gz[z] = mine.astype(BF16)
    gz_copies = []
    for k in range(1, nz):
        to = (z + k) % nz
        gz_copies.append(push(gz.at[z], gz.at[z], gzs.at[k], gzr.at[k], y * nz + to, f))
    remote_back(0, 0)
    remote_back(5, 1)
    relay(2, -back_down[2])
    relay(3, back_up[2])
    for copy in gz_copies:
        copy.wait_recv()
    mine = gz[0].astype(F32)
    for k in range(1, nz):
        mine = mine + gz[k].astype(F32)
    gfin[y] = mine.astype(BF16)
    ga_copies = []
    for k in range(1, ny):
        to = (y + k) % ny
        ga_copies.append(push(gfin.at[y], gfin.at[y], gas.at[k], gar.at[k], to * nz + z, f))
    remote_back(1, 2)
    remote_back(4, 3)
    relay(4, 0)
    remote_back(2, 4)
    relay(5, 0)
    remote_back(3, 5)
    for copy in ga_copies:
        copy.wait_recv()
    result = gfin[...].reshape(2 * width, gfin.shape[2]).astype(F32)
    gs[...] = result[:width]
    gn[...] = result[width:]
    for copy in fwd + early + back + gy_copies + gz_copies + ga_copies:
        copy.wait_send()


def body(
    features,
    w_self,
    w_neigh,
    degree,
    local_vals,
    local_dst,
    local_src,
    remote_vals,
    remote_dst,
    remote_src,
    cotangent,
):
    rows, width = features.shape
    blk = local_vals.shape[-1]
    nb = rows // blk
    rounds, per = remote_vals.shape[1:3]
    wide = w_self.shape[1]
    nd = lax.axis_size("dom")
    nf = lax.axis_size("feat")
    ny = nd // Z_CHIPS
    offsets = [(step + 1) * nd // (rounds + 1) for step in range(rounds)]
    slab = 2 * width // ny
    dma = pltpu.SemaphoreType.DMA
    vmem = pl.BlockSpec(memory_space=pltpu.VMEM)
    smem = pl.BlockSpec(memory_space=pltpu.SMEM)
    blocks = (nb, width, blk)
    out, gx, gs, gn = pl.pallas_call(
        functools.partial(kernel, nd, nf, offsets),
        out_shape=(
            jax.ShapeDtypeStruct((width, rows), BF16),
            jax.ShapeDtypeStruct((width, rows), F32),
            jax.ShapeDtypeStruct((width, wide), F32),
            jax.ShapeDtypeStruct((width, wide), F32),
        ),
        in_specs=[smem] * 4 + [vmem] * 7,
        out_specs=(vmem,) * 4,
        scratch_shapes=[
            pltpu.VMEM(blocks, BF16),
            pltpu.VMEM((2,) + blocks, F32),
            pltpu.VMEM(blocks, F32),
            pltpu.VMEM((per, width, blk), F32),
            pltpu.VMEM((6,) + blocks, BF16),
            pltpu.VMEM((6,) + blocks, BF16),
            pltpu.VMEM((nf, width, 2 * width), BF16),
            pltpu.VMEM((nf, width, 2 * width), BF16),
            pltpu.VMEM((2, width, nf * width), BF16),
            pltpu.VMEM((nf, width, rows), BF16),
            pltpu.VMEM((nf, width, rows), BF16),
            pltpu.VMEM((nf, width, rows), BF16),
            pltpu.VMEM(blocks, BF16),
        ]
        + [pltpu.VMEM(blocks, BF16)] * 6
        + [
            pltpu.VMEM((ny, slab, wide), BF16),
            pltpu.VMEM((ny, slab, wide), BF16),
            pltpu.VMEM((Z_CHIPS, slab, wide), BF16),
            pltpu.VMEM((ny, slab, wide), BF16),
            pltpu.VMEM((width, rows), F32),
            dma((6,)),
            dma((6,)),
            dma((6,)),
            dma((6,)),
            dma((nf,)),
            dma((nf,)),
            dma((nf,)),
            dma((nf,)),
            dma((9,)),
            dma((9,)),
            dma((9,)),
            dma((9,)),
            dma((ny,)),
            dma((ny,)),
            dma((Z_CHIPS,)),
            dma((Z_CHIPS,)),
            dma((ny,)),
            dma((ny,)),
        ],
        compiler_params=pltpu.CompilerParams(
            collective_id=0, has_side_effects=True, vmem_limit_bytes=40 * 1024 * 1024
        ),
    )(
        local_dst,
        local_src,
        remote_dst[0],
        remote_src[0],
        features.T,
        cotangent.T,
        w_self,
        w_neigh,
        degree.reshape(1, rows),
        local_vals[0],
        remote_vals[0],
    )
    return out.T, gx.T, gs, gn


def solution(mesh):
    placed = (
        P("dom", "feat"),
        P("feat", None),
        P("feat", None),
        P("dom"),
        P("dom", None, None, None),
        P("dom", None),
        P("dom", None),
        P("dom", None, None, None, None),
        P("dom", None, None),
        P("dom", None, None),
        P("dom", "feat"),
    )
    return jax.shard_map(
        body,
        mesh=mesh,
        in_specs=placed,
        out_specs=(P("dom", "feat"), P("dom", "feat"), P("feat", None), P("feat", None)),
        check_vma=False,
    )
```

```python
import functools

import jax
import jax.numpy as jnp
from jax import lax
from jax.experimental import pallas as pl
from jax.experimental.pallas import tpu as pltpu
from jax.sharding import PartitionSpec as P

Z_CHIPS = 12
CORES = 2
CUTS = 2
MESH = pl.DeviceIdType.MESH
F32 = jnp.float32
BF16 = jnp.bfloat16


def kernel(nd, nf, offsets, *refs):
    ins, refs = refs[:11], refs[11:]
    (out, gx, gs, gn), refs = refs[:4], refs[4:]
    held, refs = refs[:11], refs[11:]
    ld, ls, rd, rs, xt, ct, ws, wn, deg, lv, rv = held
    (
        xb,
        accs,
        loc,
        parts,
        psend,
        precv,
        wt,
        wrecv,
        wsn,
        xfull,
        afull,
        dfull,
        dsb,
        dr0,
        dr1,
        dr2,
        dr3,
        dr4,
        dr5,
        gsend,
        gyrecv,
        gz,
        gfin,
        pre,
        load_in,
        load_rv,
        fs,
        fr,
        bs,
        br,
        wss,
        wsr,
        xs,
        xr,
        as_,
        ar,
        ds,
        dr,
        gys,
        gyr,
        gzs,
        gzr,
        gas,
        gar,
    ) = refs
    loads = {}
    for r in (2, 3):
        loads["rv", r] = pltpu.make_async_copy(ins[10].at[r], rv.at[r], load_rv.at[r])
    for i in (2, 3, 4):
        loads[i] = pltpu.make_async_copy(ins[i], held[i], load_in.at[i])
    for key in (2, 3, 4, ("rv", 2), ("rv", 3)):
        loads[key].start()
    for i in (0, 1, 6, 7, 9, 8, 5):
        loads[i] = pltpu.make_async_copy(ins[i], held[i], load_in.at[i])
    for r in (1, 4, 0, 5):
        loads["rv", r] = pltpu.make_async_copy(ins[10].at[r], rv.at[r], load_rv.at[r])
    for key in (6, 7, ("rv", 1), ("rv", 4), ("rv", 0), ("rv", 5), 0, 1, 9, 8, 5):
        loads[key].start()

    def ready(*keys):
        for key in keys:
            loads[key].wait()

    width, rows = xt.shape
    nb = xb.shape[0]
    blk = xb.shape[2]
    drecv = [dr0, dr1, dr2, dr3, dr4, dr5]
    per = rv.shape[1]
    nz = Z_CHIPS
    ny = nd // nz
    nx = nf // CORES
    o = offsets
    me = lax.axis_index("dom")
    f = lax.axis_index("feat")
    y, z = me // nz, me % nz
    x, c = f // CORES, f % CORES
    f_sib = x * CORES + (CORES - 1 - c)
    f_left = ((x + nx - 1) % nx) * CORES + c
    f_right = ((x + 1) % nx) * CORES + c
    f_opp = ((x + 2) % nx) * CORES + c

    def dom_at(by):
        return (me + by + nd) % nd

    up = [o[2] - o[1], o[1] - o[0], o[0]]
    down = [o[4] - o[3], o[5] - o[4], nd - o[5]]

    barrier = pltpu.get_barrier_semaphore()
    near = sorted({h % nd for h in up + down} | {(nd - h) % nd for h in up + down})
    partners = [(dom_at(h), f) for h in near]
    partners += [(me, (f + k) % nf) for k in range(1, nf)]
    partners += [(y * nz + (z + k) % nz, f) for k in range(1, nz)]
    partners += [(((y + k) % ny) * nz + z, f) for k in range(1, ny)]
    for partner in partners:
        pl.semaphore_signal(barrier, inc=1, device_id=partner, device_id_type=MESH)

    def push(src, dst, send, recv, dom, feat):
        copy = pltpu.make_async_remote_copy(
            src_ref=src,
            dst_ref=dst,
            send_sem=send,
            recv_sem=recv,
            device_id=(dom, feat),
            device_id_type=MESH,
        )
        copy.start()
        return copy

    def collect(vals, first, pick, put, blocks, dims, acc):
        for t in range(per):
            parts[t] = lax.dot_general(
                blocks[pick[t]], vals[first + t], dims, preferred_element_type=F32
            )
        for b in range(nb):
            total = jnp.zeros((width, blk), F32)
            for t in range(per):
                total = total + jnp.where(put[t] == b, parts[t], 0.0)
            acc(b, total)

    def remote_forward(r, acc):
        collect(
            rv.at[r],
            0,
            [rs[r, 0, t] for t in range(per)],
            [rd[r, 0, t] for t in range(per)],
            xb,
            (((1,), (1,)), ((), ())),
            acc,
        )

    def to_send(k):
        def put(b, total):
            psend[k, b] = total.astype(BF16)

        return put

    def to_acc(k):
        def put(b, total):
            accs[k, b] = total

        return put

    span = nb // CUTS

    def hop(src, dst, send, recv, k, by):
        return [
            push(
                src.at[pl.ds(j * span, span)],
                dst.at[pl.ds(j * span, span)],
                send.at[k, j],
                recv.at[k, j],
                dom_at(by),
                f,
            )
            for j in range(CUTS)
        ]

    quarter = width // 4

    class Ring:

        def __init__(self, full, send, recv):
            self.full, self.send, self.recv = full, send, recv
            self.copies, self.used = [], 0

        def go(self, which, feat, low, parts_):
            part = self.full.at[which, pl.ds(low * quarter, parts_ * quarter)]
            k = self.used
            self.used += 1
            copy = push(part, part, self.send.at[k], self.recv.at[k], me, feat)
            self.copies.append(copy)
            return copy

        def start(self):
            if nx > 1:
                self.left, self.right = {}, {}
                for low, high in ((0, 2), (1, 3), (2, 0), (3, 1)):
                    self.left[low] = self.go(f, f_right, low, 1)
                    self.right[high] = self.go(f, f_left, high, 1)
            self.sib = [self.go(f, f_sib, 0, 4)]

        def middle(self):
            if nx == 1:
                return
            self.opp = []
            for low in (0, 1):
                self.left[low].wait_recv()
                self.opp.append((low, self.go(f_left, f_right, low, 1)))
                self.right[low + 2].wait_recv()
                self.opp.append((low + 2, self.go(f_right, f_left, low + 2, 1)))
            self.sib.append(self.go(f_left, f_sib, 0, 2))
            self.sib.append(self.go(f_right, f_sib, 2, 2))
            for low in (2, 3):
                self.left[low].wait_recv()
                self.right[low - 2].wait_recv()
            self.sib.append(self.go(f_left, f_sib, 2, 2))
            self.sib.append(self.go(f_right, f_sib, 0, 2))

        def last(self):
            if nx == 1:
                return
            for low, copy in self.opp:
                copy.wait_recv()
                self.sib.append(self.go(f_opp, f_sib, low, 1))

        def finish(self):
            for copy in self.sib:
                copy.wait_recv()
            for copy in self.copies:
                copy.wait_send()

    ready(2, 3, 4)
    for b in range(nb):
        xb[b] = xt[:, b * blk : (b + 1) * blk]
    xfull[f] = xt[...]
    ready(("rv", 2))
    remote_forward(2, to_send(0))
    ready(("rv", 3))
    remote_forward(3, to_send(1))
    pl.semaphore_wait(barrier, len(partners))

    fwd = [None] * 6
    fwd[0] = hop(psend.at[0], precv.at[0], fs, fr, 0, up[0])
    fwd[1] = hop(psend.at[1], precv.at[1], fs, fr, 1, -down[0])

    x_ring = Ring(xfull, xs, xr)
    x_ring.start()
    ready(6, 7)
    for q in range(ws.shape[1] // blk):
        cols = jnp.concatenate(
            [ws[:, q * blk : (q + 1) * blk], wn[:, q * blk : (q + 1) * blk]], axis=0
        )
        turned = cols.T
        for h in range(blk // width):
            wt[q * (blk // width) + h] = turned[h * width : (h + 1) * width]
    wrecv[f] = wt[f]
    early = []
    for k in range(1, nf):
        to = (f + k) % nf
        early.append(push(wt.at[to], wrecv.at[f], wss.at[k], wsr.at[k], me, to))

    ready(("rv", 1), ("rv", 4))
    remote_forward(1, to_acc(0))
    remote_forward(4, to_acc(1))

    def add_on(step, ups):
        for side in (0, 1):
            fwd[step + side] = []
        for j in range(CUTS):
            part = pl.ds(j * span, span)
            for side in (0, 1):
                k = step + side
                fwd[k - 2][j].wait_recv()
                psend[k, part] = (accs[side, part] + precv[k - 2, part].astype(F32)).astype(BF16)
                fwd[k].append(
                    push(
                        psend.at[k, part],
                        precv.at[k, part],
                        fs.at[k, j],
                        fr.at[k, j],
                        dom_at(ups[side]),
                        f,
                    )
                )

    add_on(2, (up[1], -down[1]))
    x_ring.middle()
    ready(("rv", 0), ("rv", 5))
    remote_forward(0, to_acc(0))
    remote_forward(5, to_acc(1))
    add_on(4, (up[2], -down[2]))
    x_ring.last()
    ready(0, 1, 9)

    def to_loc(b, total):
        loc[b] = total

    def add_loc(b, total):
        loc[b] = loc[b] + total

    for g in range(lv.shape[0] // per):
        collect(
            lv,
            g * per,
            [ls[0, g * per + t] for t in range(per)],
            [ld[0, g * per + t] for t in range(per)],
            xb,
            (((1,), (1,)), ((), ())),
            add_loc if g else to_loc,
        )
    for copy in early:
        copy.wait_recv()
    x_ring.finish()
    pair = blk // width
    for half, dst in ((0, 0), (1, 1)):
        for q in range(nf // pair):
            wsn[dst, :, q * blk : (q + 1) * blk] = jnp.concatenate(
                [wrecv[q * pair + h][:, half * width : (half + 1) * width] for h in range(pair)],
                axis=1,
            )
    pre[...] = jnp.dot(
        wsn[0], xfull[...].reshape(nf * width, rows), preferred_element_type=F32
    )
    ready(8, 5)
    inverse = 1.0 / deg[...].astype(F32)
    for j in range(CUTS):
        fwd[4][j].wait_recv()
        fwd[5][j].wait_recv()
        for b in range(j * span, (j + 1) * span):
            sums = loc[b] + precv[4, b].astype(F32) + precv[5, b].astype(F32)
            afull[f, :, b * blk : (b + 1) * blk] = (
                sums * inverse[:, b * blk : (b + 1) * blk]
            ).astype(BF16)

    def gather(full, send, recv):
        ring = Ring(full, send, recv)
        ring.start()
        ring.middle()
        ring.last()
        ring.finish()

    gather(afull, as_, ar)
    total = pre[...] + jnp.dot(
        wsn[1], afull[...].reshape(nf * width, rows), preferred_element_type=F32
    )
    sigma = 1.0 / (1.0 + jnp.exp(-total))
    out[...] = (total * sigma).astype(BF16)
    dfull[f] = (ct[...].astype(F32) * sigma * (1.0 + total * (1.0 - sigma))).astype(BF16)

    gather(dfull, ds, dr)
    dall = dfull[...].reshape(nf * width, rows)
    back = [[], []] + [None] * 4
    back_down = [o[0], o[1] - o[0], o[2] - o[1]]
    back_up = [nd - o[5], o[5] - o[4], o[4] - o[3]]
    for j in range(CUTS):
        low, high = j * span * blk, (j + 1) * span * blk
        dagg = jnp.dot(wn[...], dall[:, low:high], preferred_element_type=F32)
        dagg = dagg * inverse[:, low:high]
        for b in range(span):
            dsb[j * span + b] = dagg[:, b * blk : (b + 1) * blk].astype(BF16)
        part = pl.ds(j * span, span)
        for side, by in ((0, -back_down[0]), (1, back_up[0])):
            back[side].append(
                push(
                    dsb.at[part],
                    drecv[side].at[part],
                    bs.at[side, j],
                    br.at[side, j],
                    dom_at(by),
                    f,
                )
            )

    grad = lax.dot_general(
        jnp.concatenate([xt[...], afull[f]], axis=0),
        dall,
        (((1,), (1,)), ((), ())),
        preferred_element_type=F32,
    )
    slab = gsend.shape[1]
    for k in range(ny):
        gsend[k] = grad[k * slab : (k + 1) * slab].astype(BF16)
    gyrecv[y] = gsend[y]
    gy_copies = []
    for k in range(1, ny):
        to = (y + k) % ny
        gy_copies.append(
            push(gsend.at[to], gyrecv.at[y], gys.at[k], gyr.at[k], to * nz + z, f)
        )

    gx[...] = jnp.dot(ws[...], dall, preferred_element_type=F32)

    def add_gx(b, total):
        gx[:, b * blk : (b + 1) * blk] = gx[:, b * blk : (b + 1) * blk] + total

    nn = (((1,), (0,)), ((), ()))
    for g in range(lv.shape[0] // per):
        collect(
            lv,
            g * per,
            [ld[0, g * per + t] for t in range(per)],
            [ls[0, g * per + t] for t in range(per)],
            dsb,
            nn,
            add_gx,
        )

    def remote_back(r, k):
        collect(
            rv.at[r],
            0,
            [rd[r, 0, t] for t in range(per)],
            [rs[r, 0, t] for t in range(per)],
            drecv[k],
            nn,
            add_gx,
        )

    def relay(k, by):
        for j in range(CUTS):
            part = pl.ds(j * span, span)
            for side in (0, 1):
                n = k + 2 + side
                back[k + side][j].wait_recv()
                if by is None:
                    continue
                if j == 0:
                    back[n] = []
                back[n].append(
                    push(
                        drecv[k + side].at[part],
                        drecv[n].at[part],
                        bs.at[n, j],
                        br.at[n, j],
                        dom_at(by[side]),
                        f,
                    )
                )

    relay(0, (-back_down[1], back_up[1]))
    for copy in gy_copies:
        copy.wait_recv()
    mine = gyrecv[0].astype(F32)
    for k in range(1, ny):
        mine = mine + gyrecv[k].astype(F32)
    gz[z] = mine.astype(BF16)
    gz_copies = []
    for k in range(1, nz):
        to = (z + k) % nz
        gz_copies.append(push(gz.at[z], gz.at[z], gzs.at[k], gzr.at[k], y * nz + to, f))
    remote_back(0, 0)
    remote_back(5, 1)
    relay(2, (-back_down[2], back_up[2]))
    remote_back(1, 2)
    remote_back(4, 3)
    for copy in gz_copies:
        copy.wait_recv()
    mine = gz[0].astype(F32)
    for k in range(1, nz):
        mine = mine + gz[k].astype(F32)
    gfin[y] = mine.astype(BF16)
    ga_copies = []
    for k in range(1, ny):
        to = (y + k) % ny
        ga_copies.append(push(gfin.at[y], gfin.at[y], gas.at[k], gar.at[k], to * nz + z, f))
    relay(4, None)
    remote_back(2, 4)
    remote_back(3, 5)
    for copy in ga_copies:
        copy.wait_recv()
    result = gfin[...].reshape(2 * width, gfin.shape[2]).astype(F32)
    gs[...] = result[:width]
    gn[...] = result[width:]
    for copy in sum(fwd + back, []) + early + gy_copies + gz_copies + ga_copies:
        copy.wait_send()


def body(
    features,
    w_self,
    w_neigh,
    degree,
    local_vals,
    local_dst,
    local_src,
    remote_vals,
    remote_dst,
    remote_src,
    cotangent,
):
    rows, width = features.shape
    blk = local_vals.shape[-1]
    nb = rows // blk
    rounds, per = remote_vals.shape[1:3]
    wide = w_self.shape[1]
    nd = lax.axis_size("dom")
    nf = lax.axis_size("feat")
    ny = nd // Z_CHIPS
    offsets = [(step + 1) * nd // (rounds + 1) for step in range(rounds)]
    slab = 2 * width // ny
    dma = pltpu.SemaphoreType.DMA
    vmem = pl.BlockSpec(memory_space=pltpu.VMEM)
    anywhere = pl.BlockSpec(memory_space=pl.ANY)
    blocks = (nb, width, blk)
    args = (
        local_dst,
        local_src,
        remote_dst.transpose(1, 0, 2),
        remote_src.transpose(1, 0, 2),
        features.T,
        cotangent.T,
        w_self,
        w_neigh,
        degree.reshape(1, rows),
        local_vals[0],
        remote_vals[0],
    )
    out, gx, gs, gn = pl.pallas_call(
        functools.partial(kernel, nd, nf, offsets),
        out_shape=(
            jax.ShapeDtypeStruct((width, rows), BF16),
            jax.ShapeDtypeStruct((width, rows), F32),
            jax.ShapeDtypeStruct((width, wide), F32),
            jax.ShapeDtypeStruct((width, wide), F32),
        ),
        in_specs=[anywhere] * 11,
        out_specs=(vmem,) * 4,
        scratch_shapes=[
            pltpu.SMEM(a.shape, jnp.int32) if k < 4 else pltpu.VMEM(a.shape, a.dtype)
            for k, a in enumerate(args)
        ]
        + [
            pltpu.VMEM(blocks, BF16),
            pltpu.VMEM((2,) + blocks, F32),
            pltpu.VMEM(blocks, F32),
            pltpu.VMEM((per, width, blk), F32),
            pltpu.VMEM((6,) + blocks, BF16),
            pltpu.VMEM((6,) + blocks, BF16),
            pltpu.VMEM((nf, width, 2 * width), BF16),
            pltpu.VMEM((nf, width, 2 * width), BF16),
            pltpu.VMEM((2, width, nf * width), BF16),
            pltpu.VMEM((nf, width, rows), BF16),
            pltpu.VMEM((nf, width, rows), BF16),
            pltpu.VMEM((nf, width, rows), BF16),
            pltpu.VMEM(blocks, BF16),
        ]
        + [pltpu.VMEM(blocks, BF16)] * 6
        + [
            pltpu.VMEM((ny, slab, wide), BF16),
            pltpu.VMEM((ny, slab, wide), BF16),
            pltpu.VMEM((Z_CHIPS, slab, wide), BF16),
            pltpu.VMEM((ny, slab, wide), BF16),
            pltpu.VMEM((width, rows), F32),
            dma((len(args),)),
            dma((rounds,)),
            dma((6, CUTS)),
            dma((6, CUTS)),
            dma((6, CUTS)),
            dma((6, CUTS)),
            dma((nf,)),
            dma((nf,)),
        ]
        + [dma((21,))] * 6
        + [
            dma((ny,)),
            dma((ny,)),
            dma((Z_CHIPS,)),
            dma((Z_CHIPS,)),
            dma((ny,)),
            dma((ny,)),
        ],
        compiler_params=pltpu.CompilerParams(
            collective_id=0, has_side_effects=True, vmem_limit_bytes=60 * 1024 * 1024
        ),
    )(*args)
    return out.T, gx.T, gs, gn


def solution(mesh):
    placed = (
        P("dom", "feat"),
        P("feat", None),
        P("feat", None),
        P("dom"),
        P("dom", None, None, None),
        P("dom", None),
        P("dom", None),
        P("dom", None, None, None, None),
        P("dom", None, None),
        P("dom", None, None),
        P("dom", "feat"),
    )
    return jax.shard_map(
        body,
        mesh=mesh,
        in_specs=placed,
        out_specs=(P("dom", "feat"), P("dom", "feat"), P("feat", None), P("feat", None)),
        check_vma=False,
    )
```

```python
import functools

import jax
import jax.numpy as jnp
from jax import lax
from jax.experimental import pallas as pl
from jax.experimental.pallas import tpu as pltpu
from jax.sharding import PartitionSpec as P

Z_CHIPS = 12
CORES = 2
CUTS = 2
Z_GROUP = 4
MESH = pl.DeviceIdType.MESH
F32 = jnp.float32
BF16 = jnp.bfloat16


def kernel(nd, nf, offsets, *refs):
    ins, refs = refs[:11], refs[11:]
    (out, gx, gs, gn), refs = refs[:4], refs[4:]
    held, refs = refs[:11], refs[11:]
    ld, ls, rd, rs, xt, ct, ws, wn, deg, lv, rv = held
    (
        xb,
        accs,
        loc,
        parts,
        psend,
        precv,
        wfull,
        wsn,
        xfull,
        afull,
        dfull,
        dsb,
        dr0,
        dr1,
        dr2,
        dr3,
        dr4,
        dr5,
        gsend,
        gyrecv,
        gz,
        gg,
        gfin,
        pre,
        load_in,
        load_rv,
        fs,
        fr,
        bs,
        br,
        wss,
        wsr,
        xs,
        xr,
        as_,
        ar,
        ds,
        dr,
        gys,
        gyr,
        gzs,
        gzr,
        ggs,
        ggr,
        gas,
        gar,
    ) = refs
    loads = {}
    for r in (2, 3):
        loads["rv", r] = pltpu.make_async_copy(ins[10].at[r], rv.at[r], load_rv.at[r])
    for i in (2, 3, 4):
        loads[i] = pltpu.make_async_copy(ins[i], held[i], load_in.at[i])
    for key in (2, 3, 4, ("rv", 2), ("rv", 3)):
        loads[key].start()
    for i in (0, 1, 6, 7, 9, 8, 5):
        loads[i] = pltpu.make_async_copy(ins[i], held[i], load_in.at[i])
    for r in (1, 4, 0, 5):
        loads["rv", r] = pltpu.make_async_copy(ins[10].at[r], rv.at[r], load_rv.at[r])
    for key in (6, 7, ("rv", 1), ("rv", 4), ("rv", 0), ("rv", 5), 0, 1, 9, 8, 5):
        loads[key].start()

    def ready(*keys):
        for key in keys:
            loads[key].wait()

    width, rows = xt.shape
    nb = xb.shape[0]
    blk = xb.shape[2]
    drecv = [dr0, dr1, dr2, dr3, dr4, dr5]
    per = rv.shape[1]
    nz = Z_CHIPS
    ny = nd // nz
    nx = nf // CORES
    o = offsets
    me = lax.axis_index("dom")
    f = lax.axis_index("feat")
    y, z = me // nz, me % nz
    x, c = f // CORES, f % CORES
    f_sib = x * CORES + (CORES - 1 - c)
    f_left = ((x + nx - 1) % nx) * CORES + c
    f_right = ((x + 1) % nx) * CORES + c
    f_opp = ((x + 2) % nx) * CORES + c

    def dom_at(by):
        return (me + by + nd) % nd

    up = [o[2] - o[1], o[1] - o[0], o[0]]
    down = [o[4] - o[3], o[5] - o[4], nd - o[5]]

    barrier = pltpu.get_barrier_semaphore()
    near = sorted({h % nd for h in up + down} | {(nd - h) % nd for h in up + down})
    partners = [(dom_at(h), f) for h in near]
    partners += [(me, to) for to in ((f_sib, f_left, f_right) if nx > 1 else (f_sib,))]
    nzg = nz // Z_GROUP
    zg, zl = z // Z_GROUP, z % Z_GROUP
    in_group = [y * nz + zg * Z_GROUP + (zl + k) % Z_GROUP for k in range(1, Z_GROUP)]
    over_groups = [y * nz + ((zg + k) % nzg) * Z_GROUP + zl for k in range(1, nzg)]
    over_y = [((y + k) % ny) * nz + z for k in range(1, ny)]
    partners += [(to, f) for to in in_group + over_groups + over_y]
    for partner in partners:
        pl.semaphore_signal(barrier, inc=1, device_id=partner, device_id_type=MESH)

    def push(src, dst, send, recv, dom, feat):
        copy = pltpu.make_async_remote_copy(
            src_ref=src,
            dst_ref=dst,
            send_sem=send,
            recv_sem=recv,
            device_id=(dom, feat),
            device_id_type=MESH,
        )
        copy.start()
        return copy

    def collect(vals, first, pick, put, blocks, dims, acc):
        for t in range(per):
            parts[t] = lax.dot_general(
                blocks[pick[t]], vals[first + t], dims, preferred_element_type=F32
            )
        for b in range(nb):
            total = jnp.zeros((width, blk), F32)
            for t in range(per):
                total = total + jnp.where(put[t] == b, parts[t], 0.0)
            acc(b, total)

    def remote_forward(r, acc):
        collect(
            rv.at[r],
            0,
            [rs[r, 0, t] for t in range(per)],
            [rd[r, 0, t] for t in range(per)],
            xb,
            (((1,), (1,)), ((), ())),
            acc,
        )

    def to_send(k):
        def put(b, total):
            psend[k, b] = total.astype(BF16)

        return put

    def to_acc(k):
        def put(b, total):
            accs[k, b] = total

        return put

    span = nb // CUTS

    def hop(src, dst, send, recv, k, by):
        return [
            push(
                src.at[pl.ds(j * span, span)],
                dst.at[pl.ds(j * span, span)],
                send.at[k, j],
                recv.at[k, j],
                dom_at(by),
                f,
            )
            for j in range(CUTS)
        ]

    class Ring:

        def __init__(self, full, send, recv):
            self.full, self.send, self.recv = full, send, recv
            self.copies, self.half = [], full.shape[1] // 2

        def go(self, which, feat, low, halves):
            part = self.full.at[which, pl.ds(low * self.half, halves * self.half)]
            k = len(self.copies)
            copy = push(part, part, self.send.at[k], self.recv.at[k], me, feat)
            self.copies.append(copy)
            return copy

        def start(self):
            if nx > 1:
                self.left, self.right = [None] * 2, [None] * 2
                for low in (0, 1):
                    self.left[low] = self.go(f, f_right, low, 1)
                    self.right[1 - low] = self.go(f, f_left, 1 - low, 1)
            self.sib = [self.go(f, f_sib, 0, 2)]

        def middle(self):
            if nx == 1:
                return
            self.left[0].wait_recv()
            self.opp = [self.go(f_left, f_right, 0, 1)]
            self.right[1].wait_recv()
            self.opp.append(self.go(f_right, f_left, 1, 1))
            self.left[1].wait_recv()
            self.sib.append(self.go(f_left, f_sib, 0, 2))
            self.right[0].wait_recv()
            self.sib.append(self.go(f_right, f_sib, 0, 2))

        def last(self):
            if nx == 1:
                return
            for low in (0, 1):
                self.opp[low].wait_recv()
                self.sib.append(self.go(f_opp, f_sib, low, 1))

        def finish(self):
            for copy in self.sib:
                copy.wait_recv()

    ready(2, 3, 4)
    for b in range(nb):
        xb[b] = xt[:, b * blk : (b + 1) * blk]
    xfull[f] = xt[...]
    ready(("rv", 2))
    remote_forward(2, to_send(0))
    ready(("rv", 3))
    remote_forward(3, to_send(1))
    pl.semaphore_wait(barrier, len(partners))

    fwd = [None] * 6
    fwd[0] = hop(psend.at[0], precv.at[0], fs, fr, 0, up[0])
    fwd[1] = hop(psend.at[1], precv.at[1], fs, fr, 1, -down[0])

    x_ring = Ring(xfull, xs, xr)
    x_ring.start()
    ready(6, 7)
    for q in range(ws.shape[1] // blk):
        cols = jnp.concatenate(
            [ws[:, q * blk : (q + 1) * blk], wn[:, q * blk : (q + 1) * blk]], axis=0
        )
        wfull[f, q * blk : (q + 1) * blk] = cols.T
    w_ring = Ring(wfull, wss, wsr)
    w_ring.start()

    ready(("rv", 1), ("rv", 4))
    remote_forward(1, to_acc(0))
    remote_forward(4, to_acc(1))

    def add_on(step, ups):
        for side in (0, 1):
            fwd[step + side] = []
        for j in range(CUTS):
            part = pl.ds(j * span, span)
            for side in (0, 1):
                k = step + side
                fwd[k - 2][j].wait_recv()
                psend[k, part] = (accs[side, part] + precv[k - 2, part].astype(F32)).astype(BF16)
                fwd[k].append(
                    push(
                        psend.at[k, part],
                        precv.at[k, part],
                        fs.at[k, j],
                        fr.at[k, j],
                        dom_at(ups[side]),
                        f,
                    )
                )

    add_on(2, (up[1], -down[1]))
    x_ring.middle()
    w_ring.middle()
    ready(("rv", 0), ("rv", 5))
    remote_forward(0, to_acc(0))
    remote_forward(5, to_acc(1))
    add_on(4, (up[2], -down[2]))
    x_ring.last()
    w_ring.last()
    ready(0, 1, 9)

    def to_loc(b, total):
        loc[b] = total

    def add_loc(b, total):
        loc[b] = loc[b] + total

    for g in range(lv.shape[0] // per):
        collect(
            lv,
            g * per,
            [ls[0, g * per + t] for t in range(per)],
            [ld[0, g * per + t] for t in range(per)],
            xb,
            (((1,), (1,)), ((), ())),
            add_loc if g else to_loc,
        )
    x_ring.finish()
    w_ring.finish()
    pair = blk // width
    mine = [wfull[g, pl.ds(f * width, width)] for g in range(nf)]
    for half in (0, 1):
        for q in range(nf // pair):
            wsn[half, :, q * blk : (q + 1) * blk] = jnp.concatenate(
                [g[:, half * width : (half + 1) * width] for g in mine[q * pair : (q + 1) * pair]],
                axis=1,
            )
    pre[...] = jnp.dot(
        wsn[0], xfull[...].reshape(nf * width, rows), preferred_element_type=F32
    )
    ready(8, 5)
    inverse = 1.0 / deg[...].astype(F32)
    a_rings = [Ring(afull.at[j], as_.at[j], ar.at[j]) for j in range(CUTS)]
    d_rings = [Ring(dfull.at[j], ds.at[j], dr.at[j]) for j in range(CUTS)]
    run = span * blk

    def aggregate(j):
        fwd[4][j].wait_recv()
        fwd[5][j].wait_recv()
        for b in range(span):
            k = j * span + b
            sums = loc[k] + precv[4, k].astype(F32) + precv[5, k].astype(F32)
            afull[j, f, :, b * blk : (b + 1) * blk] = (
                sums * inverse[:, k * blk : (k + 1) * blk]
            ).astype(BF16)
        a_rings[j].start()

    def activate(j):
        a_rings[j].finish()
        low, high = j * run, (j + 1) * run
        total = pre[:, low:high] + jnp.dot(
            wsn[1], afull[j].reshape(nf * width, run), preferred_element_type=F32
        )
        sigma = 1.0 / (1.0 + jnp.exp(-total))
        dfull[j, f] = (
            ct[:, low:high].astype(F32) * sigma * (1.0 + total * (1.0 - sigma))
        ).astype(BF16)
        d_rings[j].start()
        out[:, low:high] = (total * sigma).astype(BF16)

    back = [[], []] + [None] * 4
    back_down = [o[0], o[1] - o[0], o[2] - o[1]]
    back_up = [nd - o[5], o[5] - o[4], o[4] - o[3]]

    def turn(j):
        d_rings[j].finish()
        low, high = j * run, (j + 1) * run
        dagg = jnp.dot(
            wn[...], dfull[j].reshape(nf * width, run), preferred_element_type=F32
        )
        dagg = dagg * inverse[:, low:high]
        for b in range(span):
            dsb[j * span + b] = dagg[:, b * blk : (b + 1) * blk].astype(BF16)
        part = pl.ds(j * span, span)
        for side, by in ((0, -back_down[0]), (1, back_up[0])):
            back[side].append(
                push(
                    dsb.at[part],
                    drecv[side].at[part],
                    bs.at[side, j],
                    br.at[side, j],
                    dom_at(by),
                    f,
                )
            )

    aggregate(0)
    aggregate(1)
    a_rings[0].middle()
    a_rings[0].last()
    a_rings[1].middle()
    activate(0)
    a_rings[1].last()
    activate(1)
    d_rings[0].middle()
    d_rings[0].last()
    d_rings[1].middle()
    turn(0)
    d_rings[1].last()
    turn(1)

    grad = jnp.zeros((2 * width, nf * width), F32)
    for j in range(CUTS):
        grad = grad + lax.dot_general(
            jnp.concatenate([xt[:, j * run : (j + 1) * run], afull[j, f]], axis=0),
            dfull[j].reshape(nf * width, run),
            (((1,), (1,)), ((), ())),
            preferred_element_type=F32,
        )
    slab = gsend.shape[1]
    for k in range(ny):
        gsend[k] = grad[k * slab : (k + 1) * slab].astype(BF16)
    gyrecv[y] = gsend[y]
    gy_copies = []
    for k in range(1, ny):
        to = (y + k) % ny
        gy_copies.append(
            push(gsend.at[to], gyrecv.at[y], gys.at[k], gyr.at[k], to * nz + z, f)
        )

    for j in range(CUTS):
        gx[:, j * run : (j + 1) * run] = jnp.dot(
            ws[...], dfull[j].reshape(nf * width, run), preferred_element_type=F32
        )

    def add_gx(b, total):
        gx[:, b * blk : (b + 1) * blk] = gx[:, b * blk : (b + 1) * blk] + total

    nn = (((1,), (0,)), ((), ()))
    for g in range(lv.shape[0] // per):
        collect(
            lv,
            g * per,
            [ld[0, g * per + t] for t in range(per)],
            [ls[0, g * per + t] for t in range(per)],
            dsb,
            nn,
            add_gx,
        )

    def remote_back(r, k):
        collect(
            rv.at[r],
            0,
            [rd[r, 0, t] for t in range(per)],
            [rs[r, 0, t] for t in range(per)],
            drecv[k],
            nn,
            add_gx,
        )

    def relay(k, j, by):
        part = pl.ds(j * span, span)
        for side in (0, 1):
            n = k + 2 + side
            back[k + side][j].wait_recv()
            if by is None:
                continue
            if j == 0:
                back[n] = []
            back[n].append(
                push(
                    drecv[k + side].at[part],
                    drecv[n].at[part],
                    bs.at[n, j],
                    br.at[n, j],
                    dom_at(by[side]),
                    f,
                )
            )

    def summed(ref):
        total = ref[0].astype(F32)
        for k in range(1, ref.shape[0]):
            total = total + ref[k].astype(F32)
        return total.astype(BF16)

    def share(ref, slot, devices, send, recv):
        return [
            push(ref.at[slot], ref.at[slot], send.at[k], recv.at[k], to, f)
            for k, to in enumerate(devices)
        ]

    relay(0, 0, (-back_down[1], back_up[1]))
    for copy in gy_copies:
        copy.wait_recv()
    gz[zl] = summed(gyrecv)
    gz_copies = share(gz, zl, in_group, gzs, gzr)
    relay(0, 1, (-back_down[1], back_up[1]))
    remote_back(0, 0)
    remote_back(5, 1)
    for copy in gz_copies:
        copy.wait_recv()
    gg[zg] = summed(gz)
    gg_copies = share(gg, zg, over_groups, ggs, ggr)
    relay(2, 0, (-back_down[2], back_up[2]))
    relay(2, 1, (-back_down[2], back_up[2]))
    remote_back(1, 2)
    remote_back(4, 3)
    for copy in gg_copies:
        copy.wait_recv()
    gfin[y] = summed(gg)
    ga_copies = share(gfin, y, over_y, gas, gar)
    relay(4, 0, None)
    relay(4, 1, None)
    remote_back(2, 4)
    remote_back(3, 5)
    for copy in ga_copies:
        copy.wait_recv()
    result = gfin[...].reshape(2 * width, gfin.shape[2]).astype(F32)
    gs[...] = result[:width]
    gn[...] = result[width:]
    rings = [x_ring, w_ring] + a_rings + d_rings
    for copy in sum(fwd + back + [ring.copies for ring in rings], []):
        copy.wait_send()
    for copy in gy_copies + gz_copies + gg_copies + ga_copies:
        copy.wait_send()


def write_out(*refs):
    n = len(refs) // 2
    copies = [pltpu.make_async_copy(refs[k], refs[n + k], refs[2 * n].at[k]) for k in range(n)]
    for copy in copies:
        copy.start()
    for copy in copies:
        copy.wait()


def body(
    features,
    w_self,
    w_neigh,
    degree,
    local_vals,
    local_dst,
    local_src,
    remote_vals,
    remote_dst,
    remote_src,
    cotangent,
):
    rows, width = features.shape
    blk = local_vals.shape[-1]
    nb = rows // blk
    rounds, per = remote_vals.shape[1:3]
    wide = w_self.shape[1]
    nd = lax.axis_size("dom")
    nf = lax.axis_size("feat")
    ny = nd // Z_CHIPS
    offsets = [(step + 1) * nd // (rounds + 1) for step in range(rounds)]
    slab = 2 * width // ny
    dma = pltpu.SemaphoreType.DMA
    vmem = pl.BlockSpec(memory_space=pltpu.VMEM)
    hbm = pl.BlockSpec(memory_space=pltpu.HBM)
    blocks = (nb, width, blk)
    args = (
        local_dst,
        local_src,
        remote_dst.transpose(1, 0, 2),
        remote_src.transpose(1, 0, 2),
        features.T,
        cotangent.T,
        w_self,
        w_neigh,
        degree.reshape(1, rows),
        local_vals[0],
        remote_vals[0],
    )
    results = pl.pallas_call(
        functools.partial(kernel, nd, nf, offsets),
        out_shape=(
            jax.ShapeDtypeStruct((width, rows), BF16),
            jax.ShapeDtypeStruct((width, rows), F32),
            jax.ShapeDtypeStruct((width, wide), F32),
            jax.ShapeDtypeStruct((width, wide), F32),
        ),
        in_specs=[hbm] * 11,
        out_specs=(vmem,) * 4,
        scratch_shapes=[
            pltpu.SMEM(a.shape, jnp.int32) if k < 4 else pltpu.VMEM(a.shape, a.dtype)
            for k, a in enumerate(args)
        ]
        + [
            pltpu.VMEM(blocks, BF16),
            pltpu.VMEM((2,) + blocks, F32),
            pltpu.VMEM(blocks, F32),
            pltpu.VMEM((per, width, blk), F32),
            pltpu.VMEM((6,) + blocks, BF16),
            pltpu.VMEM((6,) + blocks, BF16),
            pltpu.VMEM((nf, wide, 2 * width), BF16),
            pltpu.VMEM((2, width, nf * width), BF16),
            pltpu.VMEM((nf, width, rows), BF16),
            pltpu.VMEM((CUTS, nf, width, rows // CUTS), BF16),
            pltpu.VMEM((CUTS, nf, width, rows // CUTS), BF16),
            pltpu.VMEM(blocks, BF16),
        ]
        + [pltpu.VMEM(blocks, BF16)] * 6
        + [
            pltpu.VMEM((ny, slab, wide), BF16),
            pltpu.VMEM((ny, slab, wide), BF16),
            pltpu.VMEM((Z_GROUP, slab, wide), BF16),
            pltpu.VMEM((Z_CHIPS // Z_GROUP, slab, wide), BF16),
            pltpu.VMEM((ny, slab, wide), BF16),
            pltpu.VMEM((width, rows), F32),
            dma((len(args),)),
            dma((rounds,)),
            dma((6, CUTS)),
            dma((6, CUTS)),
            dma((6, CUTS)),
            dma((6, CUTS)),
        ]
        + [dma((11,))] * 4
        + [dma((CUTS, 11))] * 4
        + [
            dma((ny,)),
            dma((ny,)),
            dma((Z_GROUP,)),
            dma((Z_GROUP,)),
            dma((Z_CHIPS // Z_GROUP,)),
            dma((Z_CHIPS // Z_GROUP,)),
            dma((ny,)),
            dma((ny,)),
        ],
        compiler_params=pltpu.CompilerParams(
            collective_id=0, has_side_effects=True, vmem_limit_bytes=60 * 1024 * 1024
        ),
    )(*args)
    out, gx, gs, gn = pl.pallas_call(
        write_out,
        out_shape=tuple(jax.ShapeDtypeStruct(r.shape, r.dtype) for r in results),
        in_specs=[hbm] * 4,
        out_specs=(hbm,) * 4,
        scratch_shapes=[dma((4,))],
        compiler_params=pltpu.CompilerParams(vmem_limit_bytes=60 * 1024 * 1024),
    )(*results)
    return out.T, gx.T, gs, gn


def solution(mesh):
    placed = (
        P("dom", "feat"),
        P("feat", None),
        P("feat", None),
        P("dom"),
        P("dom", None, None, None),
        P("dom", None),
        P("dom", None),
        P("dom", None, None, None, None),
        P("dom", None, None),
        P("dom", None, None),
        P("dom", "feat"),
    )
    return jax.shard_map(
        body,
        mesh=mesh,
        in_specs=placed,
        out_specs=(P("dom", "feat"), P("dom", "feat"), P("feat", None), P("feat", None)),
        check_vma=False,
    )
```

```python
import functools

import jax
import jax.numpy as jnp
from jax import lax
from jax.experimental import pallas as pl
from jax.experimental.pallas import tpu as pltpu
from jax.sharding import PartitionSpec as P

Z_CHIPS = 12
CORES = 2
CUTS = 2
Z_GROUP = 4
MESH = pl.DeviceIdType.MESH
F32 = jnp.float32
BF16 = jnp.bfloat16


def kernel(nd, nf, offsets, *refs):
    ins, refs = refs[:11], refs[11:]
    (out, gx, gs, gn), refs = refs[:4], refs[4:]
    held, refs = refs[:11], refs[11:]
    ld, ls, rd, rs, xt, ct, ws, wn, deg, lv, rv = held
    (
        xb,
        accs,
        loc,
        parts,
        psend,
        precv,
        xw,
        xz,
        cw,
        cz,
        wall,
        wt,
        asend,
        az,
        aggt,
        osend,
        ow,
        dsend,
        dw,
        dfull,
        dall,
        dsb,
        dr0,
        dr1,
        dr2,
        dr3,
        dr4,
        dr5,
        gsend,
        gyrecv,
        gz,
        gg,
        gfin,
        pre,
        load_in,
        load_rv,
        fs,
        fr,
        bs,
        br,
        wss,
        wsr,
        ds,
        dr,
        xs,
        xr,
        cs,
        cr,
        as_,
        ar,
        os_,
        or_,
        es,
        er,
        gys,
        gyr,
        gzs,
        gzr,
        ggs,
        ggr,
        gas,
        gar,
    ) = refs
    loads = {}
    for r in (2, 3):
        loads["rv", r] = pltpu.make_async_copy(ins[10].at[r], rv.at[r], load_rv.at[r])
    for i in (2, 3, 4):
        loads[i] = pltpu.make_async_copy(ins[i], held[i], load_in.at[i])
    for key in (2, 3, 4, ("rv", 2), ("rv", 3)):
        loads[key].start()
    for i in (0, 1, 6, 7, 9, 8, 5):
        loads[i] = pltpu.make_async_copy(ins[i], held[i], load_in.at[i])
    for r in (1, 4, 0, 5):
        loads["rv", r] = pltpu.make_async_copy(ins[10].at[r], rv.at[r], load_rv.at[r])
    for key in (6, 7, ("rv", 1), ("rv", 4), ("rv", 0), ("rv", 5), 0, 1, 9, 8, 5):
        loads[key].start()

    def ready(*keys):
        for key in keys:
            loads[key].wait()

    width, rows = xt.shape
    nb = xb.shape[0]
    blk = xb.shape[2]
    drecv = [dr0, dr1, dr2, dr3, dr4, dr5]
    per = rv.shape[1]
    nz = Z_CHIPS
    ny = nd // nz
    nx = nf // CORES
    o = offsets
    me = lax.axis_index("dom")
    f = lax.axis_index("feat")
    y, z = me // nz, me % nz
    x, c = f // CORES, f % CORES
    f_sib = x * CORES + (CORES - 1 - c)
    f_left = ((x + nx - 1) % nx) * CORES + c
    f_right = ((x + 1) % nx) * CORES + c
    f_opp = ((x + 2) % nx) * CORES + c

    def dom_at(by):
        return (me + by + nd) % nd

    up = [o[2] - o[1], o[1] - o[0], o[0]]
    down = [o[4] - o[3], o[5] - o[4], nd - o[5]]

    barrier = pltpu.get_barrier_semaphore()
    near = sorted({h % nd for h in up + down} | {(nd - h) % nd for h in up + down})
    partners = [(dom_at(h), f) for h in near]
    partners += [(me, (f + k) % nf) for k in range(1, nf)]
    nzg = nz // Z_GROUP
    zg, zl = z // Z_GROUP, z % Z_GROUP
    in_group = [y * nz + zg * Z_GROUP + (zl + k) % Z_GROUP for k in range(1, Z_GROUP)]
    over_groups = [y * nz + ((zg + k) % nzg) * Z_GROUP + zl for k in range(1, nzg)]
    over_y = [((y + k) % ny) * nz + z for k in range(1, ny)]
    partners += [(to, f) for to in in_group + over_groups + over_y]
    for partner in partners:
        pl.semaphore_signal(barrier, inc=1, device_id=partner, device_id_type=MESH)

    def push(src, dst, send, recv, dom, feat):
        copy = pltpu.make_async_remote_copy(
            src_ref=src,
            dst_ref=dst,
            send_sem=send,
            recv_sem=recv,
            device_id=(dom, feat),
            device_id_type=MESH,
        )
        copy.start()
        return copy

    def collect(vals, first, pick, put, blocks, dims, acc):
        for t in range(per):
            parts[t] = lax.dot_general(
                blocks[pick[t]], vals[first + t], dims, preferred_element_type=F32
            )
        for b in range(nb):
            total = jnp.zeros((width, blk), F32)
            for t in range(per):
                total = total + jnp.where(put[t] == b, parts[t], 0.0)
            acc(b, total)

    def remote_forward(r, acc):
        collect(
            rv.at[r],
            0,
            [rs[r, 0, t] for t in range(per)],
            [rd[r, 0, t] for t in range(per)],
            xb,
            (((1,), (1,)), ((), ())),
            acc,
        )

    def to_send(k):
        def put(b, total):
            psend[k, b] = total.astype(BF16)

        return put

    def to_acc(k):
        def put(b, total):
            accs[k, b] = total

        return put

    span = nb // CUTS

    def hop(src, dst, send, recv, k, by):
        return [
            push(
                src.at[pl.ds(j * span, span)],
                dst.at[pl.ds(j * span, span)],
                send.at[k, j],
                recv.at[k, j],
                dom_at(by),
                f,
            )
            for j in range(CUTS)
        ]

    class Ring:

        def __init__(self, full, send, recv):
            self.full, self.send, self.recv = full, send, recv
            self.copies, self.half = [], full.shape[1] // 2

        def go(self, which, feat, low, halves):
            part = self.full.at[which, pl.ds(low * self.half, halves * self.half)]
            k = len(self.copies)
            copy = push(part, part, self.send.at[k], self.recv.at[k], me, feat)
            self.copies.append(copy)
            return copy

        def start(self):
            if nx > 1:
                self.left, self.right = [None] * 2, [None] * 2
                for low in (0, 1):
                    self.left[low] = self.go(f, f_right, low, 1)
                    self.right[1 - low] = self.go(f, f_left, 1 - low, 1)
            self.sib = [self.go(f, f_sib, 0, 2)]

        def middle(self):
            if nx == 1:
                return
            self.left[0].wait_recv()
            self.opp = [self.go(f_left, f_right, 0, 1)]
            self.right[1].wait_recv()
            self.opp.append(self.go(f_right, f_left, 1, 1))
            self.left[1].wait_recv()
            self.sib.append(self.go(f_left, f_sib, 0, 2))
            self.right[0].wait_recv()
            self.sib.append(self.go(f_right, f_sib, 0, 2))

        def last(self):
            if nx == 1:
                return
            for low in (0, 1):
                self.opp[low].wait_recv()
                self.sib.append(self.go(f_opp, f_sib, low, 1))

        def finish(self):
            for copy in self.sib:
                copy.wait_recv()

    wide = rows // nf
    per_dev = wide // blk

    def exchange(src, dst, send, recv):
        dst[f] = src[f]
        return [
            push(src.at[(f + k) % nf], dst.at[f], send.at[k], recv.at[k], me, (f + k) % nf)
            for k in range(1, nf)
        ]

    def arrive(copies):
        for copy in copies:
            copy.wait_recv()

    ready(2, 3, 4)
    for b in range(nb):
        xb[b] = xt[:, b * blk : (b + 1) * blk]
    ready(("rv", 2))
    remote_forward(2, to_send(0))
    pl.semaphore_wait(barrier, len(partners))
    fwd = [None] * 6
    fwd[0] = hop(psend.at[0], precv.at[0], fs, fr, 0, up[0])
    ready(("rv", 3))
    remote_forward(3, to_send(1))
    fwd[1] = hop(psend.at[1], precv.at[1], fs, fr, 1, -down[0])

    ready(6, 7, 5)
    wall[f, :width] = ws[...]
    wall[f, width:] = wn[...]
    w_ring = Ring(wall, wss, wsr)
    w_ring.start()
    for g in range(nf):
        xw[g] = xt[:, g * wide : (g + 1) * wide]
        cw[g] = ct[:, g * wide : (g + 1) * wide]
    x_copies = exchange(xw, xz, xs, xr)
    c_copies = exchange(cw, cz, cs, cr)

    ready(("rv", 1), ("rv", 4))
    remote_forward(1, to_acc(0))
    remote_forward(4, to_acc(1))

    def add_on(step, ups):
        for side in (0, 1):
            fwd[step + side] = []
        for j in range(CUTS):
            part = pl.ds(j * span, span)
            for side in (0, 1):
                k = step + side
                fwd[k - 2][j].wait_recv()
                psend[k, part] = (accs[side, part] + precv[k - 2, part].astype(F32)).astype(BF16)
                fwd[k].append(
                    push(
                        psend.at[k, part],
                        precv.at[k, part],
                        fs.at[k, j],
                        fr.at[k, j],
                        dom_at(ups[side]),
                        f,
                    )
                )

    add_on(2, (up[1], -down[1]))
    w_ring.middle()
    ready(("rv", 0), ("rv", 5))
    remote_forward(0, to_acc(0))
    remote_forward(5, to_acc(1))
    add_on(4, (up[2], -down[2]))
    w_ring.last()
    ready(0, 1, 9)

    def to_loc(b, total):
        loc[b] = total

    def add_loc(b, total):
        loc[b] = loc[b] + total

    for g in range(lv.shape[0] // per):
        collect(
            lv,
            g * per,
            [ls[0, g * per + t] for t in range(per)],
            [ld[0, g * per + t] for t in range(per)],
            xb,
            (((1,), (1,)), ((), ())),
            add_loc if g else to_loc,
        )
    w_ring.finish()
    pair = blk // width
    for half in (0, 1):
        for q in range(nf // pair):
            rows_in = jnp.concatenate(
                [wall[q * pair + h, half * width : (half + 1) * width] for h in range(pair)], axis=0
            )
            wt[half, :, q * blk : (q + 1) * blk] = rows_in.T
    arrive(x_copies)
    pre[...] = jnp.dot(wt[0], xz[...].reshape(nf * width, wide), preferred_element_type=F32)
    arrive(c_copies)
    ready(8)
    inverse = 1.0 / deg[...].astype(F32)
    for j in range(CUTS):
        arrive([fwd[4][j], fwd[5][j]])
        for b in range(j * span, (j + 1) * span):
            sums = loc[b] + precv[4, b].astype(F32) + precv[5, b].astype(F32)
            piece = (sums * inverse[:, b * blk : (b + 1) * blk]).astype(BF16)
            aggt[:, b * blk : (b + 1) * blk] = piece
            at = (b % per_dev) * blk
            asend[b // per_dev, :, at : at + blk] = piece
    a_copies = exchange(asend, az, as_, ar)
    arrive(a_copies)
    total = pre[...] + jnp.dot(
        wt[1], az[...].reshape(nf * width, wide), preferred_element_type=F32
    )
    sigma = 1.0 / (1.0 + jnp.exp(-total))
    dpre = (
        cz[...].reshape(nf * width, wide).astype(F32) * sigma * (1.0 + total * (1.0 - sigma))
    ).astype(BF16)
    own = 1.0 / deg[:, pl.ds(pl.multiple_of(f * wide, blk), wide)].astype(F32)
    dagg = jnp.dot(
        wall[:, width:, :].reshape(nf * width, nf * width), dpre, preferred_element_type=F32
    )
    dsend[...] = (dagg * own).astype(BF16).reshape(nf, width, wide)
    e_copies = exchange(dsend, dw, es, er)
    dfull[f] = dpre
    d_ring = Ring(dfull, ds, dr)
    d_ring.start()
    osend[...] = (total * sigma).astype(BF16).reshape(nf, width, wide)
    o_copies = exchange(osend, ow, os_, or_)

    back = [[], []] + [None] * 4
    back_down = [o[0], o[1] - o[0], o[2] - o[1]]
    back_up = [nd - o[5], o[5] - o[4], o[4] - o[3]]
    arrive(e_copies)
    for b in range(nb):
        at = (b % per_dev) * blk
        dsb[b] = dw[b // per_dev, :, at : at + blk]
    back[0] = hop(dsb, drecv[0], bs, br, 0, -back_down[0])
    back[1] = hop(dsb, drecv[1], bs, br, 1, back_up[0])
    d_ring.middle()
    d_ring.last()
    d_ring.finish()
    for g in range(nf):
        dall[:, g * wide : (g + 1) * wide] = dfull[g]
    grad = lax.dot_general(
        jnp.concatenate([xt[...], aggt[...]], axis=0),
        dall[...],
        (((1,), (1,)), ((), ())),
        preferred_element_type=F32,
    )
    slab = gsend.shape[1]
    for k in range(ny):
        gsend[k] = grad[k * slab : (k + 1) * slab].astype(BF16)
    gyrecv[y] = gsend[y]
    gy_copies = []
    for k in range(1, ny):
        to = (y + k) % ny
        gy_copies.append(
            push(gsend.at[to], gyrecv.at[y], gys.at[k], gyr.at[k], to * nz + z, f)
        )

    gx[...] = jnp.dot(ws[...], dall[...], preferred_element_type=F32)
    arrive(o_copies)
    for g in range(nf):
        out[:, g * wide : (g + 1) * wide] = ow[g]

    def add_gx(b, total):
        gx[:, b * blk : (b + 1) * blk] = gx[:, b * blk : (b + 1) * blk] + total

    nn = (((1,), (0,)), ((), ()))
    for g in range(lv.shape[0] // per):
        collect(
            lv,
            g * per,
            [ld[0, g * per + t] for t in range(per)],
            [ls[0, g * per + t] for t in range(per)],
            dsb,
            nn,
            add_gx,
        )

    def remote_back(r, k):
        collect(
            rv.at[r],
            0,
            [rd[r, 0, t] for t in range(per)],
            [rs[r, 0, t] for t in range(per)],
            drecv[k],
            nn,
            add_gx,
        )

    def relay(k, j, by):
        part = pl.ds(j * span, span)
        for side in (0, 1):
            n = k + 2 + side
            back[k + side][j].wait_recv()
            if by is None:
                continue
            if j == 0:
                back[n] = []
            back[n].append(
                push(
                    drecv[k + side].at[part],
                    drecv[n].at[part],
                    bs.at[n, j],
                    br.at[n, j],
                    dom_at(by[side]),
                    f,
                )
            )

    def summed(ref):
        total = ref[0].astype(F32)
        for k in range(1, ref.shape[0]):
            total = total + ref[k].astype(F32)
        return total.astype(BF16)

    def share(ref, slot, devices, send, recv):
        return [
            push(ref.at[slot], ref.at[slot], send.at[k], recv.at[k], to, f)
            for k, to in enumerate(devices)
        ]

    relay(0, 0, (-back_down[1], back_up[1]))
    for copy in gy_copies:
        copy.wait_recv()
    gz[zl] = summed(gyrecv)
    gz_copies = share(gz, zl, in_group, gzs, gzr)
    relay(0, 1, (-back_down[1], back_up[1]))
    remote_back(0, 0)
    remote_back(5, 1)
    for copy in gz_copies:
        copy.wait_recv()
    gg[zg] = summed(gz)
    gg_copies = share(gg, zg, over_groups, ggs, ggr)
    relay(2, 0, (-back_down[2], back_up[2]))
    relay(2, 1, (-back_down[2], back_up[2]))
    remote_back(1, 2)
    remote_back(4, 3)
    for copy in gg_copies:
        copy.wait_recv()
    gfin[y] = summed(gg)
    ga_copies = share(gfin, y, over_y, gas, gar)
    relay(4, 0, None)
    relay(4, 1, None)
    remote_back(2, 4)
    remote_back(3, 5)
    for copy in ga_copies:
        copy.wait_recv()
    result = gfin[...].reshape(2 * width, gfin.shape[2]).astype(F32)
    gs[...] = result[:width]
    gn[...] = result[width:]
    for copy in sum(fwd + back + [w_ring.copies, d_ring.copies], []):
        copy.wait_send()
    for copy in x_copies + c_copies + a_copies + e_copies + o_copies:
        copy.wait_send()
    for copy in gy_copies + gz_copies + gg_copies + ga_copies:
        copy.wait_send()


def write_out(*refs):
    ins, outs, held, sems = refs[:4], refs[4:8], refs[8:12], refs[12]
    fetch = [pltpu.make_async_copy(ins[k], held[k], sems.at[0, k]) for k in range(4)]
    store = [pltpu.make_async_copy(held[k], outs[k], sems.at[1, k]) for k in range(4)]
    for k in range(4):
        fetch[k].start()
    for k in range(4):
        fetch[k].wait()
        store[k].start()
    for k in range(4):
        store[k].wait()


def body(
    features,
    w_self,
    w_neigh,
    degree,
    local_vals,
    local_dst,
    local_src,
    remote_vals,
    remote_dst,
    remote_src,
    cotangent,
):
    rows, width = features.shape
    blk = local_vals.shape[-1]
    nb = rows // blk
    rounds, per = remote_vals.shape[1:3]
    wide = w_self.shape[1]
    nd = lax.axis_size("dom")
    nf = lax.axis_size("feat")
    ny = nd // Z_CHIPS
    offsets = [(step + 1) * nd // (rounds + 1) for step in range(rounds)]
    slab = 2 * width // ny
    dma = pltpu.SemaphoreType.DMA
    vmem = pl.BlockSpec(memory_space=pltpu.VMEM)
    hbm = pl.BlockSpec(memory_space=pltpu.HBM)
    blocks = (nb, width, blk)
    args = (
        local_dst,
        local_src,
        remote_dst.transpose(1, 0, 2),
        remote_src.transpose(1, 0, 2),
        features.T,
        cotangent.T,
        w_self,
        w_neigh,
        degree.reshape(1, rows),
        local_vals[0],
        remote_vals[0],
    )
    results = pl.pallas_call(
        functools.partial(kernel, nd, nf, offsets),
        out_shape=(
            jax.ShapeDtypeStruct((width, rows), BF16),
            jax.ShapeDtypeStruct((width, rows), F32),
            jax.ShapeDtypeStruct((width, wide), F32),
            jax.ShapeDtypeStruct((width, wide), F32),
        ),
        in_specs=[hbm] * 11,
        out_specs=(vmem,) * 4,
        scratch_shapes=[
            pltpu.SMEM(a.shape, jnp.int32) if k < 4 else pltpu.VMEM(a.shape, a.dtype)
            for k, a in enumerate(args)
        ]
        + [
            pltpu.VMEM(blocks, BF16),
            pltpu.VMEM((2,) + blocks, F32),
            pltpu.VMEM(blocks, F32),
            pltpu.VMEM((per, width, blk), F32),
            pltpu.VMEM((6,) + blocks, BF16),
            pltpu.VMEM((6,) + blocks, BF16),
        ]
        + [pltpu.VMEM((nf, width, rows // nf), BF16)] * 4
        + [
            pltpu.VMEM((nf, 2 * width, wide), BF16),
            pltpu.VMEM((2, wide, nf * width), BF16),
            pltpu.VMEM((nf, width, rows // nf), BF16),
            pltpu.VMEM((nf, width, rows // nf), BF16),
            pltpu.VMEM((width, rows), BF16),
        ]
        + [pltpu.VMEM((nf, width, rows // nf), BF16)] * 4
        + [
            pltpu.VMEM((nf, wide, rows // nf), BF16),
            pltpu.VMEM((wide, rows), BF16),
            pltpu.VMEM(blocks, BF16),
        ]
        + [pltpu.VMEM(blocks, BF16)] * 6
        + [
            pltpu.VMEM((ny, slab, wide), BF16),
            pltpu.VMEM((ny, slab, wide), BF16),
            pltpu.VMEM((Z_GROUP, slab, wide), BF16),
            pltpu.VMEM((Z_CHIPS // Z_GROUP, slab, wide), BF16),
            pltpu.VMEM((ny, slab, wide), BF16),
            pltpu.VMEM((wide, rows // nf), F32),
            dma((len(args),)),
            dma((rounds,)),
            dma((6, CUTS)),
            dma((6, CUTS)),
            dma((6, CUTS)),
            dma((6, CUTS)),
        ]
        + [dma((11,))] * 4
        + [dma((nf,))] * 10
        + [
            dma((ny,)),
            dma((ny,)),
            dma((Z_GROUP,)),
            dma((Z_GROUP,)),
            dma((Z_CHIPS // Z_GROUP,)),
            dma((Z_CHIPS // Z_GROUP,)),
            dma((ny,)),
            dma((ny,)),
        ],
        compiler_params=pltpu.CompilerParams(
            collective_id=0, has_side_effects=True, vmem_limit_bytes=60 * 1024 * 1024
        ),
    )(*args)
    out, gx, gs, gn = pl.pallas_call(
        write_out,
        out_shape=tuple(jax.ShapeDtypeStruct(r.shape, r.dtype) for r in results),
        in_specs=[hbm] * 4,
        out_specs=(hbm,) * 4,
        scratch_shapes=[pltpu.VMEM(r.shape, r.dtype) for r in results] + [dma((2, 4))],
        compiler_params=pltpu.CompilerParams(vmem_limit_bytes=60 * 1024 * 1024),
    )(*results)
    return out.T, gx.T, gs, gn


def solution(mesh):
    placed = (
        P("dom", "feat"),
        P("feat", None),
        P("feat", None),
        P("dom"),
        P("dom", None, None, None),
        P("dom", None),
        P("dom", None),
        P("dom", None, None, None, None),
        P("dom", None, None),
        P("dom", None, None),
        P("dom", "feat"),
    )
    return jax.shard_map(
        body,
        mesh=mesh,
        in_specs=placed,
        out_specs=(P("dom", "feat"), P("dom", "feat"), P("feat", None), P("feat", None)),
        check_vma=False,
    )
```

```python
import functools

import jax
import jax.numpy as jnp
from jax import lax
from jax.experimental import pallas as pl
from jax.experimental.pallas import tpu as pltpu
from jax.sharding import PartitionSpec as P

Z_CHIPS = 12
CORES = 2
CUTS = 2
Z_GROUP = 4
MESH = pl.DeviceIdType.MESH
F32 = jnp.float32
BF16 = jnp.bfloat16


def kernel(nd, nf, offsets, *refs):
    ins, refs = refs[:11], refs[11:]
    (out, gx, gs, gn), refs = refs[:4], refs[4:]
    held, refs = refs[:11], refs[11:]
    ld, ls, rd, rs, xt, ct, ws, wn, deg, lv, rv = held
    (
        xb,
        accs,
        loc,
        parts,
        psend,
        precv,
        xw,
        xz,
        cw,
        cz,
        wall,
        wt,
        asend,
        az,
        aggt,
        osend,
        ow,
        dsend,
        dw,
        dfull,
        dall,
        dsb,
        dr0,
        dr1,
        dr2,
        dr3,
        dr4,
        dr5,
        gsend,
        gyrecv,
        gz,
        gg,
        gfin,
        pre,
        load_in,
        load_rv,
        fs,
        fr,
        bs,
        br,
        wss,
        wsr,
        ds,
        dr,
        xs,
        xr,
        cs,
        cr,
        as_,
        ar,
        os_,
        or_,
        es,
        er,
        gys,
        gyr,
        gzs,
        gzr,
        ggs,
        ggr,
        gas,
        gar,
    ) = refs
    loads = {}
    for r in (2, 3):
        loads["rv", r] = pltpu.make_async_copy(ins[10].at[r], rv.at[r], load_rv.at[r])
    for i in (2, 3, 4):
        loads[i] = pltpu.make_async_copy(ins[i], held[i], load_in.at[i])
    for key in (2, 3, 4, ("rv", 2), ("rv", 3)):
        loads[key].start()
    def ready(*keys):
        for key in keys:
            loads[key].wait()

    width, rows = xt.shape
    nb = xb.shape[0]
    blk = xb.shape[2]
    drecv = [dr0, dr1, dr2, dr3, dr4, dr5]
    per = rv.shape[1]
    nz = Z_CHIPS
    ny = nd // nz
    nx = nf // CORES
    o = offsets
    me = lax.axis_index("dom")
    f = lax.axis_index("feat")
    y, z = me // nz, me % nz
    x, c = f // CORES, f % CORES
    f_sib = x * CORES + (CORES - 1 - c)
    f_left = ((x + nx - 1) % nx) * CORES + c
    f_right = ((x + 1) % nx) * CORES + c
    f_opp = ((x + 2) % nx) * CORES + c

    def dom_at(by):
        return (me + by + nd) % nd

    up = [o[2] - o[1], o[1] - o[0], o[0]]
    down = [o[4] - o[3], o[5] - o[4], nd - o[5]]

    barrier = pltpu.get_barrier_semaphore()
    near = sorted({h % nd for h in up + down} | {(nd - h) % nd for h in up + down})
    partners = [(dom_at(h), f) for h in near]
    partners += [(me, (f + k) % nf) for k in range(1, nf)]
    nzg = nz // Z_GROUP
    zg, zl = z // Z_GROUP, z % Z_GROUP
    in_group = [y * nz + zg * Z_GROUP + (zl + k) % Z_GROUP for k in range(1, Z_GROUP)]
    over_groups = [y * nz + ((zg + k) % nzg) * Z_GROUP + zl for k in range(1, nzg)]
    over_y = [((y + k) % ny) * nz + z for k in range(1, ny)]
    partners += [(to, f) for to in in_group + over_groups + over_y]
    for partner in partners:
        pl.semaphore_signal(barrier, inc=1, device_id=partner, device_id_type=MESH)

    for i in (0, 1, 6, 7, 9, 8, 5):
        loads[i] = pltpu.make_async_copy(ins[i], held[i], load_in.at[i])
    for r in (1, 4, 0, 5):
        loads["rv", r] = pltpu.make_async_copy(ins[10].at[r], rv.at[r], load_rv.at[r])
    for key in (6, 7, ("rv", 1), ("rv", 4), ("rv", 0), ("rv", 5), 0, 1, 9, 8, 5):
        loads[key].start()

    def push(src, dst, send, recv, dom, feat):
        copy = pltpu.make_async_remote_copy(
            src_ref=src,
            dst_ref=dst,
            send_sem=send,
            recv_sem=recv,
            device_id=(dom, feat),
            device_id_type=MESH,
        )
        copy.start()
        return copy

    def collect(vals, first, pick, put, blocks, dims, acc):
        for t in range(per):
            parts[t] = lax.dot_general(
                blocks[pick[t]], vals[first + t], dims, preferred_element_type=F32
            )
        for b in range(nb):
            total = jnp.zeros((width, blk), F32)
            for t in range(per):
                total = total + jnp.where(put[t] == b, parts[t], 0.0)
            acc(b, total)

    def remote_forward(r, acc):
        collect(
            rv.at[r],
            0,
            [rs[r, 0, t] for t in range(per)],
            [rd[r, 0, t] for t in range(per)],
            xb,
            (((1,), (1,)), ((), ())),
            acc,
        )

    def to_send(k):
        def put(b, total):
            psend[k, b] = total.astype(BF16)

        return put

    def to_acc(k):
        def put(b, total):
            accs[k, b] = total

        return put

    span = nb // CUTS

    def hop(src, dst, send, recv, k, by):
        return [
            push(
                src.at[pl.ds(j * span, span)],
                dst.at[pl.ds(j * span, span)],
                send.at[k, j],
                recv.at[k, j],
                dom_at(by),
                f,
            )
            for j in range(CUTS)
        ]

    class Ring:

        def __init__(self, full, send, recv):
            self.full, self.send, self.recv = full, send, recv
            self.copies, self.half = [], full.shape[1] // 2

        def go(self, which, feat, low, halves):
            part = self.full.at[which, pl.ds(low * self.half, halves * self.half)]
            k = len(self.copies)
            copy = push(part, part, self.send.at[k], self.recv.at[k], me, feat)
            self.copies.append(copy)
            return copy

        def start(self):
            if nx > 1:
                self.left, self.right = [None] * 2, [None] * 2
                for low in (0, 1):
                    self.left[low] = self.go(f, f_right, low, 1)
                    self.right[1 - low] = self.go(f, f_left, 1 - low, 1)
            self.sib = [self.go(f, f_sib, 0, 2)]

        def middle(self):
            if nx == 1:
                return
            self.left[0].wait_recv()
            self.opp = [self.go(f_left, f_right, 0, 1)]
            self.right[1].wait_recv()
            self.opp.append(self.go(f_right, f_left, 1, 1))
            self.left[1].wait_recv()
            self.sib.append(self.go(f_left, f_sib, 0, 2))
            self.right[0].wait_recv()
            self.sib.append(self.go(f_right, f_sib, 0, 2))

        def last(self):
            if nx == 1:
                return
            for low in (0, 1):
                self.opp[low].wait_recv()
                self.sib.append(self.go(f_opp, f_sib, low, 1))

        def finish(self):
            for copy in self.sib:
                copy.wait_recv()

    wide = rows // nf
    per_dev = wide // blk

    def exchange(src, dst, send, recv):
        dst[f] = src[f]
        return [
            push(src.at[(f + k) % nf], dst.at[f], send.at[k], recv.at[k], me, (f + k) % nf)
            for k in range(1, nf)
        ]

    def arrive(copies):
        for copy in copies:
            copy.wait_recv()

    ready(2, 3, 4)
    for b in range(nb):
        xb[b] = xt[:, b * blk : (b + 1) * blk]
    ready(("rv", 2))
    remote_forward(2, to_send(0))
    pl.semaphore_wait(barrier, len(partners))
    fwd = [None] * 6
    fwd[0] = hop(psend.at[0], precv.at[0], fs, fr, 0, up[0])
    ready(("rv", 3))
    remote_forward(3, to_send(1))
    fwd[1] = hop(psend.at[1], precv.at[1], fs, fr, 1, -down[0])

    ready(6, 7, 5)
    wall[f, :width] = ws[...]
    wall[f, width:] = wn[...]
    w_ring = Ring(wall, wss, wsr)
    w_ring.start()
    for g in range(nf):
        xw[g] = xt[:, g * wide : (g + 1) * wide]
        cw[g] = ct[:, g * wide : (g + 1) * wide]
    x_copies = exchange(xw, xz, xs, xr)
    c_copies = exchange(cw, cz, cs, cr)

    ready(("rv", 1), ("rv", 4))
    remote_forward(1, to_acc(0))
    remote_forward(4, to_acc(1))

    def add_on(step, ups):
        for side in (0, 1):
            fwd[step + side] = []
        for j in range(CUTS):
            part = pl.ds(j * span, span)
            for side in (0, 1):
                k = step + side
                fwd[k - 2][j].wait_recv()
                psend[k, part] = (accs[side, part] + precv[k - 2, part].astype(F32)).astype(BF16)
                fwd[k].append(
                    push(
                        psend.at[k, part],
                        precv.at[k, part],
                        fs.at[k, j],
                        fr.at[k, j],
                        dom_at(ups[side]),
                        f,
                    )
                )

    add_on(2, (up[1], -down[1]))
    w_ring.middle()
    ready(("rv", 0), ("rv", 5))
    remote_forward(0, to_acc(0))
    remote_forward(5, to_acc(1))
    add_on(4, (up[2], -down[2]))
    w_ring.last()
    ready(0, 1, 9)

    def to_loc(b, total):
        loc[b] = total

    def add_loc(b, total):
        loc[b] = loc[b] + total

    for g in range(lv.shape[0] // per):
        collect(
            lv,
            g * per,
            [ls[0, g * per + t] for t in range(per)],
            [ld[0, g * per + t] for t in range(per)],
            xb,
            (((1,), (1,)), ((), ())),
            add_loc if g else to_loc,
        )
    w_ring.finish()
    pair = blk // width
    for half in (0, 1):
        for q in range(nf // pair):
            rows_in = jnp.concatenate(
                [wall[q * pair + h, half * width : (half + 1) * width] for h in range(pair)], axis=0
            )
            wt[half, :, q * blk : (q + 1) * blk] = rows_in.T
    arrive(x_copies)
    pre[...] = jnp.dot(wt[0], xz[...].reshape(nf * width, wide), preferred_element_type=F32)
    arrive(c_copies)
    ready(8)
    inverse = 1.0 / deg[...].astype(F32)
    for j in range(CUTS):
        arrive([fwd[4][j], fwd[5][j]])
        for b in range(j * span, (j + 1) * span):
            sums = loc[b] + precv[4, b].astype(F32) + precv[5, b].astype(F32)
            piece = (sums * inverse[:, b * blk : (b + 1) * blk]).astype(BF16)
            aggt[:, b * blk : (b + 1) * blk] = piece
            at = (b % per_dev) * blk
            asend[b // per_dev, :, at : at + blk] = piece
    a_copies = exchange(asend, az, as_, ar)
    arrive(a_copies)
    total = pre[...] + jnp.dot(
        wt[1], az[...].reshape(nf * width, wide), preferred_element_type=F32
    )
    sigma = 1.0 / (1.0 + jnp.exp(-total))
    dpre = (
        cz[...].reshape(nf * width, wide).astype(F32) * sigma * (1.0 + total * (1.0 - sigma))
    ).astype(BF16)
    own = 1.0 / deg[:, pl.ds(pl.multiple_of(f * wide, blk), wide)].astype(F32)
    dagg = jnp.dot(
        wall[:, width:, :].reshape(nf * width, nf * width), dpre, preferred_element_type=F32
    )
    dsend[...] = (dagg * own).astype(BF16).reshape(nf, width, wide)
    e_copies = exchange(dsend, dw, es, er)
    dfull[f] = dpre
    d_ring = Ring(dfull, ds, dr)
    d_ring.start()
    osend[...] = (total * sigma).astype(BF16).reshape(nf, width, wide)

    back = [[], []] + [None] * 4
    back_down = [o[0], o[1] - o[0], o[2] - o[1]]
    back_up = [nd - o[5], o[5] - o[4], o[4] - o[3]]
    arrive(e_copies)
    for b in range(nb):
        at = (b % per_dev) * blk
        dsb[b] = dw[b // per_dev, :, at : at + blk]
    back[0] = hop(dsb, drecv[0], bs, br, 0, -back_down[0])
    back[1] = hop(dsb, drecv[1], bs, br, 1, back_up[0])
    def relay(k, j, by):
        part = pl.ds(j * span, span)
        for side in (0, 1):
            n = k + 2 + side
            back[k + side][j].wait_recv()
            if by is None:
                continue
            if j == 0:
                back[n] = []
            back[n].append(
                push(
                    drecv[k + side].at[part],
                    drecv[n].at[part],
                    bs.at[n, j],
                    br.at[n, j],
                    dom_at(by[side]),
                    f,
                )
            )

    first, second = (-back_down[1], back_up[1]), (-back_down[2], back_up[2])
    d_ring.middle()
    d_ring.last()
    relay(0, 0, first)
    d_ring.finish()
    for g in range(nf):
        dall[:, g * wide : (g + 1) * wide] = dfull[g]
    grad = lax.dot_general(
        jnp.concatenate([xt[...], aggt[...]], axis=0),
        dall[...],
        (((1,), (1,)), ((), ())),
        preferred_element_type=F32,
    )
    slab = gsend.shape[1]
    for k in range(ny):
        gsend[k] = grad[k * slab : (k + 1) * slab].astype(BF16)
    gyrecv[y] = gsend[y]
    gy_copies = []
    for k in range(1, ny):
        to = (y + k) % ny
        gy_copies.append(
            push(gsend.at[to], gyrecv.at[y], gys.at[k], gyr.at[k], to * nz + z, f)
        )

    for j in range(1, CUTS):
        relay(0, j, first)
    o_copies = exchange(osend, ow, os_, or_)
    gx[...] = jnp.dot(ws[...], dall[...], preferred_element_type=F32)

    def add_gx(b, total):
        gx[:, b * blk : (b + 1) * blk] = gx[:, b * blk : (b + 1) * blk] + total

    nn = (((1,), (0,)), ((), ()))
    for g in range(lv.shape[0] // per):
        collect(
            lv,
            g * per,
            [ld[0, g * per + t] for t in range(per)],
            [ls[0, g * per + t] for t in range(per)],
            dsb,
            nn,
            add_gx,
        )

    def remote_back(r, k):
        collect(
            rv.at[r],
            0,
            [rd[r, 0, t] for t in range(per)],
            [rs[r, 0, t] for t in range(per)],
            drecv[k],
            nn,
            add_gx,
        )

    def summed(ref):
        total = ref[0].astype(F32)
        for k in range(1, ref.shape[0]):
            total = total + ref[k].astype(F32)
        return total.astype(BF16)

    def share(ref, slot, devices, send, recv):
        return [
            push(ref.at[slot], ref.at[slot], send.at[k], recv.at[k], to, f)
            for k, to in enumerate(devices)
        ]

    arrive(gy_copies)
    gz[zl] = summed(gyrecv)
    gz_copies = share(gz, zl, in_group, gzs, gzr)
    remote_back(0, 0)
    remote_back(5, 1)
    for j in range(CUTS):
        relay(2, j, second)
    arrive(gz_copies)
    gg[zg] = summed(gz)
    gg_copies = share(gg, zg, over_groups, ggs, ggr)
    remote_back(1, 2)
    remote_back(4, 3)
    arrive(o_copies)
    for g in range(nf):
        out[:, g * wide : (g + 1) * wide] = ow[g]
    arrive(gg_copies)
    gfin[y] = summed(gg)
    ga_copies = share(gfin, y, over_y, gas, gar)
    for j in range(CUTS):
        relay(4, j, None)
    remote_back(2, 4)
    remote_back(3, 5)
    arrive(ga_copies)
    result = gfin[...].reshape(2 * width, gfin.shape[2]).astype(F32)
    gs[...] = result[:width]
    gn[...] = result[width:]
    for copy in sum(fwd + back + [w_ring.copies, d_ring.copies], []):
        copy.wait_send()
    for copy in x_copies + c_copies + a_copies + e_copies + o_copies:
        copy.wait_send()
    for copy in gy_copies + gz_copies + gg_copies + ga_copies:
        copy.wait_send()


def write_out(*refs):
    copies = [pltpu.make_async_copy(refs[k], refs[4 + k], refs[8].at[k]) for k in range(4)]
    for copy in copies:
        copy.start()
    for copy in copies:
        copy.wait()


def body(
    features,
    w_self,
    w_neigh,
    degree,
    local_vals,
    local_dst,
    local_src,
    remote_vals,
    remote_dst,
    remote_src,
    cotangent,
):
    rows, width = features.shape
    blk = local_vals.shape[-1]
    nb = rows // blk
    rounds, per = remote_vals.shape[1:3]
    wide = w_self.shape[1]
    nd = lax.axis_size("dom")
    nf = lax.axis_size("feat")
    ny = nd // Z_CHIPS
    offsets = [(step + 1) * nd // (rounds + 1) for step in range(rounds)]
    slab = 2 * width // ny
    dma = pltpu.SemaphoreType.DMA
    vmem = pl.BlockSpec(memory_space=pltpu.VMEM)
    hbm = pl.BlockSpec(memory_space=pltpu.HBM)
    blocks = (nb, width, blk)
    args = (
        local_dst,
        local_src,
        remote_dst.transpose(1, 0, 2),
        remote_src.transpose(1, 0, 2),
        features.T,
        cotangent.T,
        w_self,
        w_neigh,
        degree.reshape(1, rows),
        local_vals[0],
        remote_vals[0],
    )
    results = pl.pallas_call(
        functools.partial(kernel, nd, nf, offsets),
        out_shape=(
            jax.ShapeDtypeStruct((width, rows), BF16),
            jax.ShapeDtypeStruct((width, rows), F32),
            jax.ShapeDtypeStruct((width, wide), F32),
            jax.ShapeDtypeStruct((width, wide), F32),
        ),
        in_specs=[hbm] * 11,
        out_specs=(vmem,) * 4,
        scratch_shapes=[
            pltpu.SMEM(a.shape, jnp.int32) if k < 4 else pltpu.VMEM(a.shape, a.dtype)
            for k, a in enumerate(args)
        ]
        + [
            pltpu.VMEM(blocks, BF16),
            pltpu.VMEM((2,) + blocks, F32),
            pltpu.VMEM(blocks, F32),
            pltpu.VMEM((per, width, blk), F32),
            pltpu.VMEM((6,) + blocks, BF16),
            pltpu.VMEM((6,) + blocks, BF16),
        ]
        + [pltpu.VMEM((nf, width, rows // nf), BF16)] * 4
        + [
            pltpu.VMEM((nf, 2 * width, wide), BF16),
            pltpu.VMEM((2, wide, nf * width), BF16),
            pltpu.VMEM((nf, width, rows // nf), BF16),
            pltpu.VMEM((nf, width, rows // nf), BF16),
            pltpu.VMEM((width, rows), BF16),
        ]
        + [pltpu.VMEM((nf, width, rows // nf), BF16)] * 4
        + [
            pltpu.VMEM((nf, wide, rows // nf), BF16),
            pltpu.VMEM((wide, rows), BF16),
            pltpu.VMEM(blocks, BF16),
        ]
        + [pltpu.VMEM(blocks, BF16)] * 6
        + [
            pltpu.VMEM((ny, slab, wide), BF16),
            pltpu.VMEM((ny, slab, wide), BF16),
            pltpu.VMEM((Z_GROUP, slab, wide), BF16),
            pltpu.VMEM((Z_CHIPS // Z_GROUP, slab, wide), BF16),
            pltpu.VMEM((ny, slab, wide), BF16),
            pltpu.VMEM((wide, rows // nf), F32),
            dma((len(args),)),
            dma((rounds,)),
            dma((6, CUTS)),
            dma((6, CUTS)),
            dma((6, CUTS)),
            dma((6, CUTS)),
        ]
        + [dma((11,))] * 4
        + [dma((nf,))] * 10
        + [
            dma((ny,)),
            dma((ny,)),
            dma((Z_GROUP,)),
            dma((Z_GROUP,)),
            dma((Z_CHIPS // Z_GROUP,)),
            dma((Z_CHIPS // Z_GROUP,)),
            dma((ny,)),
            dma((ny,)),
        ],
        compiler_params=pltpu.CompilerParams(
            collective_id=0, has_side_effects=True, vmem_limit_bytes=32 * 1024 * 1024
        ),
    )(*[pltpu.with_memory_space_constraint(a, pltpu.HBM) for a in args])
    out, gx, gs, gn = pl.pallas_call(
        write_out,
        out_shape=tuple(jax.ShapeDtypeStruct(r.shape, r.dtype) for r in results),
        in_specs=[vmem] * 4,
        out_specs=(hbm,) * 4,
        scratch_shapes=[dma((4,))],
        compiler_params=pltpu.CompilerParams(vmem_limit_bytes=16 * 1024 * 1024),
    )(*results)
    return out.T, gx.T, gs, gn


def solution(mesh):
    placed = (
        P("dom", "feat"),
        P("feat", None),
        P("feat", None),
        P("dom"),
        P("dom", None, None, None),
        P("dom", None),
        P("dom", None),
        P("dom", None, None, None, None),
        P("dom", None, None),
        P("dom", None, None),
        P("dom", "feat"),
    )
    return jax.shard_map(
        body,
        mesh=mesh,
        in_specs=placed,
        out_specs=(P("dom", "feat"), P("dom", "feat"), P("feat", None), P("feat", None)),
        check_vma=False,
    )
```

```python
import functools

import jax
import jax.numpy as jnp
from jax import lax
from jax.experimental import pallas as pl
from jax.experimental.pallas import tpu as pltpu
from jax.sharding import PartitionSpec as P

Z_CHIPS = 12
CORES = 2
CUTS = 2
Z_GROUP = 4
MESH = pl.DeviceIdType.MESH
F32 = jnp.float32
BF16 = jnp.bfloat16


def kernel(nd, nf, offsets, *refs):
    ins, refs = refs[:11], refs[11:]
    (out, gx, gs, gn), refs = refs[:4], refs[4:]
    held, refs = refs[:11], refs[11:]
    ld, ls, rd, rs, xt, ct, ws, wn, deg, lv, rv = held
    (
        xb,
        accs,
        loc,
        parts,
        psend,
        precv,
        xw,
        xz,
        cw,
        cz,
        wall,
        wt,
        asend,
        az,
        aggt,
        osend,
        ow,
        dsend,
        dw,
        dfull,
        dall,
        dsb,
        dr0,
        dr1,
        dr2,
        dr3,
        dr4,
        dr5,
        gsend,
        gyrecv,
        gz,
        gg,
        gfin,
        pre,
        load_in,
        load_rv,
        fs,
        fr,
        bs,
        br,
        wss,
        wsr,
        ds,
        dr,
        xs,
        xr,
        cs,
        cr,
        as_,
        ar,
        os_,
        or_,
        es,
        er,
        gys,
        gyr,
        gzs,
        gzr,
        ggs,
        ggr,
        gas,
        gar,
    ) = refs
    loads = {}
    for r in (2, 3):
        loads["rv", r] = pltpu.make_async_copy(ins[10].at[r], rv.at[r], load_rv.at[r])
    for i in (2, 3, 4):
        loads[i] = pltpu.make_async_copy(ins[i], held[i], load_in.at[i])
    for key in (2, 3, 4, ("rv", 2), ("rv", 3)):
        loads[key].start()
    def ready(*keys):
        for key in keys:
            loads[key].wait()

    width, rows = xt.shape
    nb = xb.shape[0]
    blk = xb.shape[2]
    drecv = [dr0, dr1, dr2, dr3, dr4, dr5]
    per = rv.shape[1]
    nz = Z_CHIPS
    ny = nd // nz
    nx = nf // CORES
    o = offsets
    me = lax.axis_index("dom")
    f = lax.axis_index("feat")
    y, z = me // nz, me % nz
    x, c = f // CORES, f % CORES
    f_sib = x * CORES + (CORES - 1 - c)
    f_left = ((x + nx - 1) % nx) * CORES + c
    f_right = ((x + 1) % nx) * CORES + c
    f_opp = ((x + 2) % nx) * CORES + c

    def dom_at(by):
        return (me + by + nd) % nd

    up = [o[2] - o[1], o[1] - o[0], o[0]]
    down = [o[4] - o[3], o[5] - o[4], nd - o[5]]

    barrier = pltpu.get_barrier_semaphore()
    near = sorted({h % nd for h in up + down} | {(nd - h) % nd for h in up + down})
    partners = [(dom_at(h), f) for h in near]
    partners += [(me, (f + k) % nf) for k in range(1, nf)]
    nzg = nz // Z_GROUP
    zg, zl = z // Z_GROUP, z % Z_GROUP
    in_group = [y * nz + zg * Z_GROUP + (zl + k) % Z_GROUP for k in range(1, Z_GROUP)]
    over_groups = [y * nz + ((zg + k) % nzg) * Z_GROUP + zl for k in range(1, nzg)]
    over_y = [((y + k) % ny) * nz + z for k in range(1, ny)]
    partners += [(to, f) for to in in_group + over_groups + over_y]
    for partner in partners:
        pl.semaphore_signal(barrier, inc=1, device_id=partner, device_id_type=MESH)

    for i in (0, 1, 6, 7, 9, 8, 5):
        loads[i] = pltpu.make_async_copy(ins[i], held[i], load_in.at[i])
    for r in (1, 4, 0, 5):
        loads["rv", r] = pltpu.make_async_copy(ins[10].at[r], rv.at[r], load_rv.at[r])
    for key in (6, 7, ("rv", 1), ("rv", 4), ("rv", 0), ("rv", 5), 0, 1, 9, 8, 5):
        loads[key].start()

    def push(src, dst, send, recv, dom, feat):
        copy = pltpu.make_async_remote_copy(
            src_ref=src,
            dst_ref=dst,
            send_sem=send,
            recv_sem=recv,
            device_id=(dom, feat),
            device_id_type=MESH,
        )
        copy.start()
        return copy

    def collect(vals, first, pick, put, blocks, dims, acc):
        for t in range(per):
            parts[t] = lax.dot_general(
                blocks[pick[t]], vals[first + t], dims, preferred_element_type=F32
            )
        for b in range(nb):
            total = jnp.zeros((width, blk), F32)
            for t in range(per):
                total = total + jnp.where(put[t] == b, parts[t], 0.0)
            acc(b, total)

    def remote_forward(r, acc):
        collect(
            rv.at[r],
            0,
            [rs[r, 0, t] for t in range(per)],
            [rd[r, 0, t] for t in range(per)],
            xb,
            (((1,), (1,)), ((), ())),
            acc,
        )

    def to_send(k):
        def put(b, total):
            psend[k, b] = total.astype(BF16)

        return put

    def to_acc(k):
        def put(b, total):
            accs[k, b] = total

        return put

    span = nb // CUTS

    def hop(src, dst, send, recv, k, by):
        return [
            push(
                src.at[pl.ds(j * span, span)],
                dst.at[pl.ds(j * span, span)],
                send.at[k, j],
                recv.at[k, j],
                dom_at(by),
                f,
            )
            for j in range(CUTS)
        ]

    class Ring:

        def __init__(self, full, send, recv):
            self.full, self.send, self.recv = full, send, recv
            self.copies, self.half = [], full.shape[1] // 2

        def go(self, which, feat, low, halves):
            part = self.full.at[which, pl.ds(low * self.half, halves * self.half)]
            k = len(self.copies)
            copy = push(part, part, self.send.at[k], self.recv.at[k], me, feat)
            self.copies.append(copy)
            return copy

        def start(self):
            if nx > 1:
                self.left, self.right = [None] * 2, [None] * 2
                for low in (0, 1):
                    self.left[low] = self.go(f, f_right, low, 1)
                    self.right[1 - low] = self.go(f, f_left, 1 - low, 1)
            self.sib = [self.go(f, f_sib, 0, 2)]

        def middle(self):
            if nx == 1:
                return
            self.left[0].wait_recv()
            self.opp = [self.go(f_left, f_right, 0, 1)]
            self.right[1].wait_recv()
            self.opp.append(self.go(f_right, f_left, 1, 1))
            self.left[1].wait_recv()
            self.sib.append(self.go(f_left, f_sib, 0, 2))
            self.right[0].wait_recv()
            self.sib.append(self.go(f_right, f_sib, 0, 2))

        def last(self):
            if nx == 1:
                return
            for low in (0, 1):
                self.opp[low].wait_recv()
                self.sib.append(self.go(f_opp, f_sib, low, 1))

        def finish(self):
            for copy in self.sib:
                copy.wait_recv()

    wide = rows // nf
    per_dev = wide // blk

    def exchange(src, dst, send, recv):
        dst[f] = src[f]
        return [
            push(src.at[(f + k) % nf], dst.at[f], send.at[k], recv.at[k], me, (f + k) % nf)
            for k in range(1, nf)
        ]

    def arrive(copies):
        for copy in copies:
            copy.wait_recv()

    ready(2, 3, 4)
    for b in range(nb):
        xb[b] = xt[:, b * blk : (b + 1) * blk]
    ready(("rv", 2))
    remote_forward(2, to_send(0))
    pl.semaphore_wait(barrier, len(partners))
    fwd = [None] * 6
    fwd[0] = hop(psend.at[0], precv.at[0], fs, fr, 0, up[0])
    ready(("rv", 3))
    remote_forward(3, to_send(1))
    fwd[1] = hop(psend.at[1], precv.at[1], fs, fr, 1, -down[0])

    ready(6, 7, 5)
    wall[f, :width] = ws[...]
    wall[f, width:] = wn[...]
    w_ring = Ring(wall, wss, wsr)
    w_ring.start()
    for g in range(nf):
        xw[g] = xt[:, g * wide : (g + 1) * wide]
        cw[g] = ct[:, g * wide : (g + 1) * wide]
    x_copies = exchange(xw, xz, xs, xr)
    c_copies = exchange(cw, cz, cs, cr)

    ready(("rv", 1), ("rv", 4))
    remote_forward(1, to_acc(0))
    remote_forward(4, to_acc(1))

    def add_on(step, ups):
        for side in (0, 1):
            fwd[step + side] = []
        for j in range(CUTS):
            part = pl.ds(j * span, span)
            for side in (0, 1):
                k = step + side
                fwd[k - 2][j].wait_recv()
                psend[k, part] = (accs[side, part] + precv[k - 2, part].astype(F32)).astype(BF16)
                fwd[k].append(
                    push(
                        psend.at[k, part],
                        precv.at[k, part],
                        fs.at[k, j],
                        fr.at[k, j],
                        dom_at(ups[side]),
                        f,
                    )
                )

    add_on(2, (up[1], -down[1]))
    w_ring.middle()
    ready(("rv", 0), ("rv", 5))
    remote_forward(0, to_acc(0))
    remote_forward(5, to_acc(1))
    add_on(4, (up[2], -down[2]))
    w_ring.last()
    ready(0, 1, 9)

    def to_loc(b, total):
        loc[b] = total

    def add_loc(b, total):
        loc[b] = loc[b] + total

    for g in range(lv.shape[0] // per):
        collect(
            lv,
            g * per,
            [ls[0, g * per + t] for t in range(per)],
            [ld[0, g * per + t] for t in range(per)],
            xb,
            (((1,), (1,)), ((), ())),
            add_loc if g else to_loc,
        )
    w_ring.finish()
    pair = blk // width
    for half in (0, 1):
        for q in range(nf // pair):
            rows_in = jnp.concatenate(
                [wall[q * pair + h, half * width : (half + 1) * width] for h in range(pair)], axis=0
            )
            wt[half, :, q * blk : (q + 1) * blk] = rows_in.T
    arrive(x_copies)
    pre[...] = jnp.dot(wt[0], xz[...].reshape(nf * width, wide), preferred_element_type=F32)
    arrive(c_copies)
    ready(8)
    inverse = 1.0 / deg[...].astype(F32)
    for j in range(CUTS):
        arrive([fwd[4][j], fwd[5][j]])
        for b in range(j * span, (j + 1) * span):
            sums = loc[b] + precv[4, b].astype(F32) + precv[5, b].astype(F32)
            piece = (sums * inverse[:, b * blk : (b + 1) * blk]).astype(BF16)
            aggt[:, b * blk : (b + 1) * blk] = piece
            at = (b % per_dev) * blk
            asend[b // per_dev, :, at : at + blk] = piece
    a_copies = exchange(asend, az, as_, ar)
    arrive(a_copies)
    total = pre[...] + jnp.dot(
        wt[1], az[...].reshape(nf * width, wide), preferred_element_type=F32
    )
    sigma = 1.0 / (1.0 + jnp.exp(-total))
    dpre = (
        cz[...].reshape(nf * width, wide).astype(F32) * sigma * (1.0 + total * (1.0 - sigma))
    ).astype(BF16)
    own = 1.0 / deg[:, pl.ds(pl.multiple_of(f * wide, blk), wide)].astype(F32)
    dagg = jnp.dot(
        wall[:, width:, :].reshape(nf * width, nf * width), dpre, preferred_element_type=F32
    )
    dsend[...] = (dagg * own).astype(BF16).reshape(nf, width, wide)
    e_copies = exchange(dsend, dw, es, er)
    dfull[f] = dpre
    d_ring = Ring(dfull, ds, dr)
    d_ring.start()
    osend[...] = (total * sigma).astype(BF16).reshape(nf, width, wide)

    back = [[], []] + [None] * 4
    back_down = [o[0], o[1] - o[0], o[2] - o[1]]
    back_up = [nd - o[5], o[5] - o[4], o[4] - o[3]]
    arrive(e_copies)
    for b in range(nb):
        at = (b % per_dev) * blk
        dsb[b] = dw[b // per_dev, :, at : at + blk]
    back[0] = hop(dsb, drecv[0], bs, br, 0, -back_down[0])
    back[1] = hop(dsb, drecv[1], bs, br, 1, back_up[0])
    def relay(k, j, by):
        part = pl.ds(j * span, span)
        for side in (0, 1):
            n = k + 2 + side
            back[k + side][j].wait_recv()
            if by is None:
                continue
            if j == 0:
                back[n] = []
            back[n].append(
                push(
                    drecv[k + side].at[part],
                    drecv[n].at[part],
                    bs.at[n, j],
                    br.at[n, j],
                    dom_at(by[side]),
                    f,
                )
            )

    first, second = (-back_down[1], back_up[1]), (-back_down[2], back_up[2])
    d_ring.middle()
    d_ring.last()
    relay(0, 0, first)
    d_ring.finish()
    for g in range(nf):
        dall[:, g * wide : (g + 1) * wide] = dfull[g]
    grad = lax.dot_general(
        jnp.concatenate([xt[...], aggt[...]], axis=0),
        dall[...],
        (((1,), (1,)), ((), ())),
        preferred_element_type=F32,
    )
    slab = gsend.shape[1]
    for k in range(ny):
        gsend[k] = grad[k * slab : (k + 1) * slab].astype(BF16)
    gyrecv[y] = gsend[y]
    gy_copies = []
    for k in range(1, ny):
        to = (y + k) % ny
        gy_copies.append(
            push(gsend.at[to], gyrecv.at[y], gys.at[k], gyr.at[k], to * nz + z, f)
        )

    for j in range(1, CUTS):
        relay(0, j, first)
    o_copies = exchange(osend, ow, os_, or_)
    gx[...] = jnp.dot(ws[...], dall[...], preferred_element_type=F32)

    def add_gx(b, total):
        gx[:, b * blk : (b + 1) * blk] = gx[:, b * blk : (b + 1) * blk] + total

    nn = (((1,), (0,)), ((), ()))
    for g in range(lv.shape[0] // per):
        collect(
            lv,
            g * per,
            [ld[0, g * per + t] for t in range(per)],
            [ls[0, g * per + t] for t in range(per)],
            dsb,
            nn,
            add_gx,
        )

    def remote_back(r, k):
        collect(
            rv.at[r],
            0,
            [rd[r, 0, t] for t in range(per)],
            [rs[r, 0, t] for t in range(per)],
            drecv[k],
            nn,
            add_gx,
        )

    def summed(ref):
        total = ref[0].astype(F32)
        for k in range(1, ref.shape[0]):
            total = total + ref[k].astype(F32)
        return total.astype(BF16)

    def share(ref, slot, devices, send, recv):
        return [
            push(ref.at[slot], ref.at[slot], send.at[k], recv.at[k], to, f)
            for k, to in enumerate(devices)
        ]

    arrive(gy_copies)
    gz[zl] = summed(gyrecv)
    gz_copies = share(gz, zl, in_group, gzs, gzr)
    remote_back(0, 0)
    remote_back(5, 1)
    relay(2, 0, second)
    arrive(gz_copies)
    gg[zg] = summed(gz)
    gg_copies = share(gg, zg, over_groups, ggs, ggr)
    for j in range(1, CUTS):
        relay(2, j, second)
    remote_back(1, 2)
    remote_back(4, 3)
    arrive(o_copies)
    for g in range(nf):
        out[:, g * wide : (g + 1) * wide] = ow[g]
    arrive(gg_copies)
    gfin[y] = summed(gg)
    ga_copies = share(gfin, y, over_y, gas, gar)
    for j in range(CUTS):
        relay(4, j, None)
    remote_back(2, 4)
    remote_back(3, 5)
    arrive(ga_copies)
    result = gfin[...].reshape(2 * width, gfin.shape[2]).astype(F32)
    gs[...] = result[:width]
    gn[...] = result[width:]
    for copy in sum(fwd + back + [w_ring.copies, d_ring.copies], []):
        copy.wait_send()
    for copy in x_copies + c_copies + a_copies + e_copies + o_copies:
        copy.wait_send()
    for copy in gy_copies + gz_copies + gg_copies + ga_copies:
        copy.wait_send()


def write_out(*refs):
    copies = [pltpu.make_async_copy(refs[k], refs[4 + k], refs[8].at[k]) for k in range(4)]
    for copy in copies:
        copy.start()
    for copy in copies:
        copy.wait()


def body(
    features,
    w_self,
    w_neigh,
    degree,
    local_vals,
    local_dst,
    local_src,
    remote_vals,
    remote_dst,
    remote_src,
    cotangent,
):
    rows, width = features.shape
    blk = local_vals.shape[-1]
    nb = rows // blk
    rounds, per = remote_vals.shape[1:3]
    wide = w_self.shape[1]
    nd = lax.axis_size("dom")
    nf = lax.axis_size("feat")
    ny = nd // Z_CHIPS
    offsets = [(step + 1) * nd // (rounds + 1) for step in range(rounds)]
    slab = 2 * width // ny
    dma = pltpu.SemaphoreType.DMA
    vmem = pl.BlockSpec(memory_space=pltpu.VMEM)
    hbm = pl.BlockSpec(memory_space=pltpu.HBM)
    blocks = (nb, width, blk)
    args = (
        local_dst,
        local_src,
        remote_dst.transpose(1, 0, 2),
        remote_src.transpose(1, 0, 2),
        features.T,
        cotangent.T,
        w_self,
        w_neigh,
        degree.reshape(1, rows),
        local_vals[0],
        remote_vals[0],
    )
    results = pl.pallas_call(
        functools.partial(kernel, nd, nf, offsets),
        out_shape=(
            jax.ShapeDtypeStruct((width, rows), BF16),
            jax.ShapeDtypeStruct((width, rows), F32),
            jax.ShapeDtypeStruct((width, wide), F32),
            jax.ShapeDtypeStruct((width, wide), F32),
        ),
        in_specs=[hbm] * 11,
        out_specs=(vmem,) * 4,
        scratch_shapes=[
            pltpu.SMEM(a.shape, jnp.int32) if k < 4 else pltpu.VMEM(a.shape, a.dtype)
            for k, a in enumerate(args)
        ]
        + [
            pltpu.VMEM(blocks, BF16),
            pltpu.VMEM((2,) + blocks, F32),
            pltpu.VMEM(blocks, F32),
            pltpu.VMEM((per, width, blk), F32),
            pltpu.VMEM((6,) + blocks, BF16),
            pltpu.VMEM((6,) + blocks, BF16),
        ]
        + [pltpu.VMEM((nf, width, rows // nf), BF16)] * 4
        + [
            pltpu.VMEM((nf, 2 * width, wide), BF16),
            pltpu.VMEM((2, wide, nf * width), BF16),
            pltpu.VMEM((nf, width, rows // nf), BF16),
            pltpu.VMEM((nf, width, rows // nf), BF16),
            pltpu.VMEM((width, rows), BF16),
        ]
        + [pltpu.VMEM((nf, width, rows // nf), BF16)] * 4
        + [
            pltpu.VMEM((nf, wide, rows // nf), BF16),
            pltpu.VMEM((wide, rows), BF16),
            pltpu.VMEM(blocks, BF16),
        ]
        + [pltpu.VMEM(blocks, BF16)] * 6
        + [
            pltpu.VMEM((ny, slab, wide), BF16),
            pltpu.VMEM((ny, slab, wide), BF16),
            pltpu.VMEM((Z_GROUP, slab, wide), BF16),
            pltpu.VMEM((Z_CHIPS // Z_GROUP, slab, wide), BF16),
            pltpu.VMEM((ny, slab, wide), BF16),
            pltpu.VMEM((wide, rows // nf), F32),
            dma((len(args),)),
            dma((rounds,)),
            dma((6, CUTS)),
            dma((6, CUTS)),
            dma((6, CUTS)),
            dma((6, CUTS)),
        ]
        + [dma((11,))] * 4
        + [dma((nf,))] * 10
        + [
            dma((ny,)),
            dma((ny,)),
            dma((Z_GROUP,)),
            dma((Z_GROUP,)),
            dma((Z_CHIPS // Z_GROUP,)),
            dma((Z_CHIPS // Z_GROUP,)),
            dma((ny,)),
            dma((ny,)),
        ],
        compiler_params=pltpu.CompilerParams(
            collective_id=0, has_side_effects=True, vmem_limit_bytes=32 * 1024 * 1024
        ),
    )(*[pltpu.with_memory_space_constraint(a, pltpu.HBM) for a in args])
    out, gx, gs, gn = pl.pallas_call(
        write_out,
        out_shape=tuple(jax.ShapeDtypeStruct(r.shape, r.dtype) for r in results),
        in_specs=[vmem] * 4,
        out_specs=(hbm,) * 4,
        scratch_shapes=[dma((4,))],
        compiler_params=pltpu.CompilerParams(vmem_limit_bytes=16 * 1024 * 1024),
    )(*results)
    return out.T, gx.T, gs, gn


def solution(mesh):
    placed = (
        P("dom", "feat"),
        P("feat", None),
        P("feat", None),
        P("dom"),
        P("dom", None, None, None),
        P("dom", None),
        P("dom", None),
        P("dom", None, None, None, None),
        P("dom", None, None),
        P("dom", None, None),
        P("dom", "feat"),
    )
    return jax.shard_map(
        body,
        mesh=mesh,
        in_specs=placed,
        out_specs=(P("dom", "feat"), P("dom", "feat"), P("feat", None), P("feat", None)),
        check_vma=False,
    )
```
